32 devices in a mesh: groups: 2 (over y), row: 4 (over x, core), col: 4 (over z).
Axes of the slice: x: 2, y: 2, z: 4, core: 2. Of those that a mesh axis runs over, the one named last changes fastest.
Arguments:
- tiles: float32 [512, 128, 128], P(('groups', 'row', 'col')), parts along dimension 0, may hold values from 0 to 9
- tile_index: int32 [512, 2], P(('groups', 'row', 'col')), parts along dimension 0, may hold values from 0 to 3, as said below
- tile_count: int32 [32], P(('groups', 'row', 'col')), parts along dimension 0, may hold values from 4 to 16, as said below
- sources: int32 [16], P('groups'), parts along dimension 0, may hold values from 0 to 2047
Outputs:
- distance: float32 [16, 2048], P('groups', ('row', 'col')), parts along dimension 0
- path_counts: float32 [16, 2048], P('groups', ('row', 'col')), parts along dimension 0
- centrality: float32 [4096], P(('groups', 'row', 'col')), parts along dimension 0
The draws below stay inside these ranges and needn't reach their ends.
There are 2 independent parts, one for each index of `groups`. The reference program is written for one: setup_inputs(seed, part) draws one part's arguments, and reference() takes and returns one part's arrays. A program takes and returns all parts, laid end to end along the dimension named above; each array names one. Nothing has to cross between parts.
Inputs may be any that keep to these rules, and one draw needn't show every extreme that they name: `tile_index`: entry (r, c) of a slot has r below 4 and c below 4; the 16 slots of one device name distinct pairs. `tile_count`: one entry per device; slots of a device from its count on hold only zeros; some device has all 16 slots live.
All inputs are finite; a program needn't handle non-finite values.
Results may differ from the reference program's by a relative error of at most 0.0003.
Values sent between devices are 32-bit elements; how exact they have to be, the bound alone decides.
A program may use at most 64 MiB of HBM per device.

```python
import jax
import jax.numpy as jnp
from jax import lax

TILE = 128
SLOTS = 16
SOURCES = 8
WMAX = 8
LEVELS = 3
BACK = 2
DEVS = 16
VERTICES = 2048
SLOT_ALL = 256
N_ROW = 4
N_COL = 4


def tile_layout(key):
    layout_key = jax.random.fold_in(key, 101)
    perm_key, count_key, pick_key, weight_key, keep_key, level_key = jax.random.split(layout_key, 6)
    placed = jax.vmap(lambda one_key: jax.random.permutation(one_key, N_ROW * N_COL)[:SLOTS])(jax.random.split(perm_key, DEVS))
    live_counts = jax.random.randint(count_key, (DEVS,), SLOTS // 4, SLOTS + 1)
    fullest = jax.random.randint(pick_key, (), 0, DEVS)
    live_counts = jnp.where(jnp.arange(DEVS) == fullest, SLOTS, live_counts).astype(jnp.int32)
    whole_parts = jax.random.randint(weight_key, (DEVS, SLOTS, TILE, TILE), 1, WMAX + 1).astype(jnp.float32)
    kept_edges = jax.random.randint(keep_key, (DEVS, SLOTS, TILE, TILE), 0, TILE) < 2
    live_slots = jnp.arange(SLOTS)[None, :] < live_counts[:, None]
    vertex_level = jax.random.randint(level_key, (VERTICES,), 0, 2 ** 17).astype(jnp.float32) * 2.0 ** (-18)
    row_tile = placed // N_ROW
    col_tile = placed % N_ROW
    dev_ids = jnp.arange(DEVS)
    row_base = (dev_ids[:, None] // N_COL * N_COL + row_tile) * TILE
    col_base = (col_tile * N_COL + dev_ids[:, None] % N_COL) * TILE
    offsets = jnp.arange(TILE)
    row_level = vertex_level[row_base[:, :, None] + offsets[None, None, :]]
    col_level = vertex_level[col_base[:, :, None] + offsets[None, None, :]]
    weights = whole_parts + col_level[:, :, None, :] - row_level[:, :, :, None]
    tile_values = jnp.where(kept_edges & live_slots[:, :, None, None], weights, 0.0).reshape(DEVS * SLOTS, TILE, TILE).astype(jnp.float32)
    positions = jnp.stack([row_tile, col_tile], axis=-1).reshape(DEVS * SLOTS, 2).astype(jnp.int32)
    return (tile_values, positions, live_counts)


def draw_tiles(key, part):
    return tile_layout(key)[0]


def draw_tile_index(key, part):
    return tile_layout(key)[1]


def draw_tile_count(key, part):
    return tile_layout(key)[2]


def place_ends(drawn, own_key, low, high):
    longest = drawn.shape.index(max(drawn.shape))
    spots = []
    for shift in (0, 1):
        where = [jax.random.randint(jax.random.fold_in(own_key, axis), (), 0, length) for axis, length in enumerate(drawn.shape)]
        where[longest] = (where[longest] + shift) % drawn.shape[longest]
        spots.append(tuple(where))
    return drawn.at[spots[0]].set(low).at[spots[1]].set(high)


def setup_inputs(seed: int = 0, part: int = 0) -> dict:
    seeds = jax.random.split(jax.random.key(seed), 5)
    part_splits = jax.random.split(jax.random.fold_in(seeds[4], part), 5)
    tiles = draw_tiles(jax.random.fold_in(jax.random.fold_in(seeds[4], part), 71), part)
    tile_index = draw_tile_index(jax.random.fold_in(jax.random.fold_in(seeds[4], part), 71), part)
    tile_count = draw_tile_count(jax.random.fold_in(jax.random.fold_in(seeds[4], part), 71), part)
    sources = place_ends(jax.random.randint(part_splits[3], (SOURCES,), 0, VERTICES), jax.random.fold_in(part_splits[3], 1), 0, VERTICES - 1).astype(jnp.int32)
    return {"tiles": tiles, "tile_index": tile_index, "tile_count": tile_count, "sources": sources}


far_value = 1.0e6
no_edge = 2.0e6


def combine_pair(left_pair, right_pair):
    best_dist = jnp.minimum(left_pair[0], right_pair[0])
    total_count = jnp.where(left_pair[0] == best_dist, left_pair[1], 0.0) + jnp.where(right_pair[0] == best_dist, right_pair[1], 0.0)
    return best_dist, total_count


def edge_weights(raw_tile):
    return jnp.where(raw_tile > 0, raw_tile.astype(jnp.float32), no_edge)


def relax_tile(near_dist, near_count, weight_tile):
    source_rows = near_dist.shape[0]
    tile_side = weight_tile.shape[0]
    block_size = min(16, tile_side)
    blocks = tile_side // block_size
    dist_blocks = near_dist.reshape(source_rows, blocks, block_size).transpose(1, 0, 2)
    count_blocks = near_count.reshape(source_rows, blocks, block_size).transpose(1, 0, 2)
    weight_blocks = weight_tile.reshape(blocks, block_size, tile_side)

    def advance(carried, pieces):
        dist_part, count_part, weight_part = pieces
        reached = dist_part[:, :, None] + weight_part[None, :, :]
        best_dist = jnp.min(reached, axis=1)
        total_count = jnp.sum(jnp.where(reached == best_dist[:, None, :], count_part[:, :, None], 0.0), axis=1)
        return combine_pair(carried, (best_dist, total_count)), None

    initial = (jnp.full((source_rows, tile_side), far_value, near_dist.dtype), jnp.zeros((source_rows, tile_side), near_dist.dtype))
    result, unused = lax.scan(advance, initial, (dist_blocks, count_blocks, weight_blocks))
    return result


def depend_tile(upper_dist, lower_dist, lower_coef, weight_tile):
    source_rows = upper_dist.shape[0]
    tile_side = weight_tile.shape[0]
    block_size = min(16, tile_side)
    blocks = tile_side // block_size
    upper_blocks = upper_dist.reshape(source_rows, blocks, block_size).transpose(1, 0, 2)
    weight_blocks = weight_tile.reshape(blocks, block_size, tile_side)

    def dependency_rows(pieces):
        upper_part, weight_part = pieces
        reached = upper_part[:, :, None] + weight_part[None, :, :]
        return jnp.sum(jnp.where(reached == lower_dist[:, None, :], lower_coef[:, None, :], 0.0), axis=2)

    row_parts = lax.map(dependency_rows, (upper_blocks, weight_blocks))
    return row_parts.transpose(1, 0, 2).reshape(source_rows, tile_side)


def reference(tiles, tile_index, tile_count, sources):
    source_rows = sources.shape[0]
    vertex_ids = jnp.arange(VERTICES, dtype=jnp.int32)
    is_source = vertex_ids[None, :] == sources[:, None]
    start_dist = jnp.where(is_source, 0.0, far_value).astype(jnp.float32)
    source_ones = jnp.where(is_source, 1.0, 0.0).astype(jnp.float32)
    distance = start_dist
    path_counts = source_ones
    slot_ids = jnp.arange(SLOT_ALL, dtype=jnp.int32)

    def place(slot_id):
        owner_dev = slot_id // SLOTS
        local_slot = slot_id % SLOTS
        row_block = owner_dev // N_COL
        col_block = owner_dev % N_COL
        row_start = ((row_block * N_COL + tile_index[slot_id, 0]) * TILE).astype(jnp.int32)
        col_start = ((tile_index[slot_id, 1] * N_COL + col_block) * TILE).astype(jnp.int32)
        return row_start, col_start, local_slot < tile_count[owner_dev]

    for level_no in range(LEVELS):
        def forward_step(carried, slot_id, distance=distance, path_counts=path_counts):
            row_start, col_start, is_live = place(slot_id)
            weight_tile = edge_weights(tiles[slot_id])

            def active(current):
                near_dist = lax.dynamic_slice_in_dim(distance, row_start, TILE, 1)
                near_count = lax.dynamic_slice_in_dim(path_counts, row_start, TILE, 1)
                found = relax_tile(near_dist, near_count, weight_tile)
                previous = (lax.dynamic_slice_in_dim(current[0], col_start, TILE, 1), lax.dynamic_slice_in_dim(current[1], col_start, TILE, 1))
                merged = combine_pair(previous, found)
                return (lax.dynamic_update_slice_in_dim(current[0], merged[0], col_start, 1), lax.dynamic_update_slice_in_dim(current[1], merged[1], col_start, 1))

            return lax.cond(is_live, active, lambda unchanged: unchanged, carried), None

        initial = (jnp.full((source_rows, VERTICES), far_value, jnp.float32), jnp.zeros((source_rows, VERTICES), jnp.float32))
        (cand_dist, cand_count), unused = lax.scan(forward_step, initial, slot_ids)
        distance = jnp.minimum(start_dist, cand_dist)
        path_counts = source_ones + jnp.where(cand_dist == distance, cand_count, 0.0)

    dependency = jnp.zeros((source_rows, VERTICES), jnp.float32)
    for back_no in range(BACK):
        coefficient = jnp.where(path_counts > 0.5, (1.0 + dependency) / jnp.maximum(path_counts, 1.0), 0.0)

        def backward_step(carried, slot_id, coefficient=coefficient):
            row_start, col_start, is_live = place(slot_id)
            weight_tile = edge_weights(tiles[slot_id])

            def active(current):
                upper_dist = lax.dynamic_slice_in_dim(distance, row_start, TILE, 1)
                lower_dist = lax.dynamic_slice_in_dim(distance, col_start, TILE, 1)
                lower_coef = lax.dynamic_slice_in_dim(coefficient, col_start, TILE, 1)
                dep_term = depend_tile(upper_dist, lower_dist, lower_coef, weight_tile)
                previous = lax.dynamic_slice_in_dim(current, row_start, TILE, 1)
                return lax.dynamic_update_slice_in_dim(current, previous + dep_term, row_start, 1)

            return lax.cond(is_live, active, lambda unchanged: unchanged, carried), None

        accumulated, unused = lax.scan(backward_step, jnp.zeros((source_rows, VERTICES), jnp.float32), slot_ids)
        dependency = path_counts * accumulated

    centrality = jnp.sum(jnp.where(is_source, 0.0, dependency), axis=0) / source_rows
    shown = jnp.where(distance < 0.5 * far_value, distance, -1.0)
    return shown, path_counts, centrality
```

```python
import functools

import jax
import jax.numpy as jnp
from jax import lax
from jax.experimental import pallas as pl
from jax.experimental.pallas import tpu as pltpu
from jax.sharding import PartitionSpec as P

LEVELS = 3
BACK = 2
CHUNK = 4
PAIR = 2
SUB = 8
MASK_TILES = 32

far_value = 1000000.0
no_edge = 2000000.0
half_far = 500000.0
scale_up = 2.0**60


def partner(me, step, count):
    if count & (count - 1):
        return (me + step) % count
    total = 0
    bit = 1
    while bit < count:
        total = total + ((me // bit) % 2 + (step // bit) % 2) % 2 * bit
        bit *= 2
    return total


def fold(parts, join, sub):
    half = SUB // 2
    while len(parts) > 1:
        low = sub % (2 * half) < half
        count = len(parts) // 2
        parts = [
            join(
                jnp.where(low, parts[k], parts[k + count]),
                pltpu.roll(jnp.where(low, parts[k + count], parts[k]), half, 0)
                if half * 2 == SUB
                else jnp.where(
                    low,
                    pltpu.roll(parts[k], SUB - half, 0),
                    pltpu.roll(parts[k + count], half, 0),
                ),
            )
            for k in range(count)
        ]
        half //= 2
    return parts[0]


def body(
    row_count,
    col_count,
    index_hbm,
    count_hbm,
    source_hbm,
    tiles_ref,
    packed,
    index_ref,
    count_ref,
    source_ref,
    raw,
    place_ref,
    weights,
    weights_back,
    pick,
    lanes,
    lanes_more,
    masks,
    gathered,
    dist_out,
    count_out,
    dist_in,
    count_in,
    full_dist,
    full_count,
    band,
    lower,
    sums_out,
    sums_all,
    sums_in,
    load_sem,
    small_sem,
    all_send,
    all_recv,
    full_send,
    full_recv,
    col_send,
    col_recv,
):
    slot_total, tile_side = raw.shape[0], raw.shape[1]
    source_rows = source_ref.shape[0]
    my_row = lax.axis_index("row")
    my_col = lax.axis_index("col")
    positions = row_count * col_count
    row_chunk = CHUNK if row_count % CHUNK == 0 else 1
    row_pair = PAIR if row_count % PAIR == 0 else 1
    col_pair = PAIR if col_count % PAIR == 0 else 1
    groups = tile_side // SUB
    wide = (source_rows, tile_side)
    last = LEVELS - 1
    keep_masks = masks.shape[0] == positions
    pending = []

    def others():
        for col_step in reversed(range(col_count)):
            for row_step in reversed(range(row_count)):
                if row_step or col_step:
                    yield (
                        partner(my_row, row_step, row_count),
                        partner(my_col, col_step, col_count),
                        row_step,
                        col_step,
                    )

    small = [
        pltpu.make_async_copy(index_hbm, index_ref, small_sem.at[0]),
        pltpu.make_async_copy(count_hbm, count_ref, small_sem.at[1]),
        pltpu.make_async_copy(source_hbm, source_ref, small_sem.at[2]),
    ]
    for copy in small:
        copy.start()
    load = pltpu.make_async_copy(tiles_ref, raw, load_sem)
    load.start()
    barrier = pltpu.get_barrier_semaphore()
    for other_row, other_col, _, _ in others():
        pl.semaphore_signal(
            barrier,
            inc=1,
            device_id={"row": other_row, "col": other_col},
            device_id_type=pl.DeviceIdType.MESH,
        )

    def start(source, target, send, recv, device):
        copy = pltpu.make_async_remote_copy(
            src_ref=source,
            dst_ref=target,
            send_sem=send,
            recv_sem=recv,
            device_id=device,
            device_id_type=pl.DeviceIdType.MESH,
        )
        copy.start()
        pending.append(copy)

    def push_all(stage, source_of, target, with_own_col=True):
        for other_row, other_col, row_step, col_step in others():
            if col_step or with_own_col:
                start(
                    source_of(other_row, other_col),
                    target,
                    all_send.at[stage, row_step, col_step],
                    all_recv.at[stage, my_row, my_col],
                    {"row": other_row, "col": other_col},
                )

    def push_full(stage, source, target):
        target[my_row] = source[...]
        for row_step in reversed(range(1, row_count)):
            start(
                source,
                target.at[my_row],
                full_send.at[stage, row_step],
                full_recv.at[stage, my_row],
                {"row": partner(my_row, row_step, row_count), "col": my_col},
            )

    def arrived(target, recv, device):
        pltpu.make_async_remote_copy(
            src_ref=target,
            dst_ref=target,
            send_sem=load_sem,
            recv_sem=recv,
            device_id=device,
            device_id_type=pl.DeviceIdType.MESH,
        ).wait_recv()

    def full_arrived(stage, target):
        for row_step in range(1, row_count):
            other = partner(my_row, row_step, row_count)
            arrived(target.at[other], full_recv.at[stage, other], {"row": other, "col": my_col})

    def block_arrived(stage, target, block, own):
        for row_step in range(row_count):
            giver = partner(my_row, row_step, row_count)

            def wait():
                arrived(
                    target.at[block, giver],
                    all_recv.at[stage, giver, block],
                    {"row": giver, "col": block},
                )

            if row_step == 0 and own is not None:
                pl.when(jnp.logical_not(own))(wait)
            else:
                wait()

    def source_mask(base):
        wanted = jnp.full(wide, -1, jnp.int32)
        for row in range(source_rows):
            wanted = jnp.where(sub == row, source_ref[row] - base, wanted)
        return lane == wanted

    def settle(found_dist, found_count, is_source):
        start_dist = jnp.where(is_source, 0.0, far_value).astype(jnp.float32)
        settled = jnp.minimum(start_dist, found_dist)
        ones = jnp.where(is_source, 1.0, 0.0).astype(jnp.float32)
        return settled, ones + jnp.where(found_dist == settled, found_count, 0.0)

    def nearest(values):
        return functools.reduce(jnp.minimum, values)

    def combine(dists, counts):
        best = nearest(dists)
        total = functools.reduce(
            jnp.add, [jnp.where(d == best, n, 0.0) for d, n in zip(dists, counts, strict=True)]
        )
        return best, total

    def spread(value, target):
        scaled = value * scale_up
        high = scaled.astype(jnp.bfloat16).astype(jnp.float32)
        rest = scaled - high
        middle = rest.astype(jnp.bfloat16).astype(jnp.float32)
        pieces = jnp.concatenate([high, middle, rest - middle, jnp.zeros_like(high)], axis=0)
        target[...] = lax.dot_general(
            pieces.astype(jnp.bfloat16),
            pick[...],
            (((0,), (0,)), ((), ())),
            preferred_element_type=jnp.float32,
        )

    def spread_at(ref, place, group, s):
        return ref[
            place, group * SUB : (group + 1) * SUB, s * tile_side : (s + 1) * tile_side
        ]

    for copy in small:
        copy.wait()
    live_count = count_ref[0]
    holds = []
    for slot in range(slot_total):
        position = index_ref[0, slot] * row_count + index_ref[1, slot]
        holds.append(jnp.where(slot < live_count, position, -1))

    def find_slot(position, carried):
        found = jnp.int32(-1)
        for slot in range(slot_total):
            found = jnp.where(holds[slot] == position, jnp.int32(slot), found)
        place_ref[position] = found
        return carried

    lax.fori_loop(0, positions, find_slot, 0)

    lane = lax.broadcasted_iota(jnp.int32, wide, 1)
    sub = lax.broadcasted_iota(jnp.int32, wide, 0)
    load.wait()

    band_base = my_row * col_count * tile_side

    part_row = lax.broadcasted_iota(jnp.int32, pick.shape, 0)
    part_source = lax.broadcasted_iota(jnp.int32, pick.shape, 1) // tile_side
    chosen = (part_row % source_rows == part_source) & (part_row < 3 * source_rows)
    pick[...] = jnp.where(chosen, 1.0 / scale_up, 0.0).astype(jnp.bfloat16)

    def first_level(column, carried):
        best = jnp.full(wide, far_value, jnp.float32)
        for row in range(source_rows):
            place = source_ref[row] - band_base
            inside = (place >= 0) & (place < col_count * tile_side)
            place = jnp.clip(place, 0, col_count * tile_side - 1)
            slot = place_ref[(place // tile_side) * row_count + column]
            line = raw[jnp.maximum(slot, 0), pl.ds(place % tile_side, 1), :]
            limit = jnp.where(inside & (slot >= 0), 0.0, far_value).astype(jnp.float32)
            best = jnp.where((sub == row) & (line > limit), line, best)
        dist_out[0, column] = best
        return carried

    lax.fori_loop(0, row_count, first_level, 0)
    dist_in[0, my_col, my_row] = dist_out[0, my_row]
    pl.semaphore_wait(barrier, row_count * col_count - 1)
    push_all(0, lambda other_row, other_col: dist_out.at[0, other_row], dist_in.at[0, my_col, my_row])

    def prepare(position, carried):
        slot = place_ref[position]
        tile = raw[jnp.maximum(slot, 0)]
        limit = jnp.where(slot >= 0, 0.0, far_value).astype(jnp.float32)
        weights[position] = jnp.where(tile > limit, tile, no_edge)
        return carried

    lax.fori_loop(0, positions, prepare, 0)

    def turn(position, carried):
        weights_back[position] = weights[position].T
        return carried

    lax.fori_loop(0, positions, turn, 0)

    def relax(block):
        def columns(chunk, carried):
            first = chunk * row_chunk
            best = [[gathered[first + t, s] for s in range(source_rows)] for t in range(row_chunk)]
            for group in range(groups):
                lines = [
                    weights[block * row_count + first + t, group * SUB : (group + 1) * SUB, :]
                    for t in range(row_chunk)
                ]
                for s in range(source_rows):
                    near = spread_at(lanes, block, group, s)
                    for t in range(row_chunk):
                        best[t][s] = jnp.minimum(best[t][s], near + lines[t])
            for t in range(row_chunk):
                for s in range(source_rows):
                    gathered[first + t, s] = best[t][s]
            return carried

        lax.fori_loop(0, row_count // row_chunk, columns, 0)

    def tally(level, block):
        def columns(chunk, carried):
            first = chunk * row_pair
            total = [[gathered[first + t, s] for s in range(source_rows)] for t in range(row_pair)]
            best = [
                [
                    jnp.broadcast_to(dist_out[level, first + t, s : s + 1, :], (SUB, tile_side))
                    for s in range(source_rows)
                ]
                for t in range(row_pair)
            ]
            for group in range(groups):
                lines = [
                    weights[block * row_count + first + t, group * SUB : (group + 1) * SUB, :]
                    for t in range(row_pair)
                ]
                for s in range(source_rows):
                    near = spread_at(lanes, block, group, s)
                    paths = 1.0 if level == 1 else spread_at(lanes_more, block, group, s)
                    for t in range(row_pair):
                        total[t][s] += jnp.where(near + lines[t] == best[t][s], paths, 0.0)
            for t in range(row_pair):
                for s in range(source_rows):
                    gathered[first + t, s] = total[t][s]
            return carried

        lax.fori_loop(0, row_count // row_pair, columns, 0)

    def fill(count, value):
        def one(place, carried):
            for s in range(source_rows):
                gathered[place, s] = jnp.full((SUB, tile_side), value, jnp.float32)
            return carried

        lax.fori_loop(0, count, one, 0)

    def forward(level):
        fill(row_count, far_value)

        def relax_block(step, carried):
            block = partner(my_col, step, col_count)
            block_arrived(level - 1, dist_in.at[level - 1], block, step == 0)
            best = nearest([dist_in[level - 1, block, g] for g in range(row_count)])
            is_source = source_mask((my_row * col_count + block) * tile_side)
            spread(jnp.where(is_source, 0.0, best), lanes.at[block])
            relax(block)
            return carried

        lax.fori_loop(0, col_count, relax_block, 0)

        def close_dist(column, carried):
            dist_out[level, column] = fold(
                [gathered[column, s] for s in range(source_rows)], jnp.minimum, sub
            )
            return carried

        lax.fori_loop(0, row_count, close_dist, 0)
        if level == last:
            push_full(0, dist_out.at[level], full_dist)
        else:
            dist_in[level, my_col, my_row] = dist_out[level, my_row]
        push_all(
            level,
            lambda other_row, other_col: dist_out.at[level, other_row],
            dist_in.at[level, my_col, my_row],
            level != last,
        )

        fill(row_count, 0.0)

        def tally_blocks(pair, carried):
            blocks = [partner(my_col, pair * col_pair + t, col_count) for t in range(col_pair)]
            if level > 1:
                for t, block in enumerate(blocks):
                    block_arrived(LEVELS, count_in, block, (pair == 0) if t == 0 else None)
                for block in blocks:
                    found = combine(
                        [dist_in[level - 1, block, g] for g in range(row_count)],
                        [count_in[block, g] for g in range(row_count)],
                    )
                    is_source = source_mask((my_row * col_count + block) * tile_side)
                    spread(settle(*found, is_source)[1], lanes_more.at[block])
            for block in blocks:
                tally(level, block)
            return carried

        lax.fori_loop(0, col_count // col_pair, tally_blocks, 0)

        def close_count(column, carried):
            total = fold([gathered[column, s] for s in range(source_rows)], jnp.add, sub)
            if level == 1:
                total = jnp.where(dist_out[level, column] < half_far, total, 0.0)
            count_out[level - 1, column] = total
            return carried

        lax.fori_loop(0, row_count, close_count, 0)
        if level == last:
            push_full(1, count_out.at[level - 1], full_count)
        else:
            count_in[my_col, my_row] = count_out[level - 1, my_row]
            push_all(
                LEVELS,
                lambda other_row, other_col: count_out.at[level - 1, other_row],
                count_in.at[my_col, my_row],
            )

    for level in range(1, LEVELS):
        forward(level)

    full_arrived(0, full_dist)

    def lower_dist(chunk, carried):
        for t in range(row_chunk):
            column = chunk * row_chunk + t
            best = nearest([full_dist[g, column] for g in range(row_count)])
            is_source = source_mask((column * col_count + my_col) * tile_side)
            settled = jnp.where(is_source, 0.0, best)
            lower[0, column] = settled
            spread(settled, lanes.at[column])
        return carried

    lax.fori_loop(0, row_count // row_chunk, lower_dist, 0)

    def settle_upper(block):
        for row_step in range(row_count):
            giver = partner(my_row, row_step, row_count)
            arrived(
                dist_in.at[last, block, giver],
                all_recv.at[last, giver, block],
                {"row": giver, "col": block},
            )
        best = nearest([dist_in[last, block, g] for g in range(row_count)])
        is_source = source_mask((my_row * col_count + block) * tile_side)
        band[block] = jnp.where(is_source, 0.0, best)

    def upper_lines(block):
        return [
            jnp.broadcast_to(band[block, s : s + 1, :], (SUB, tile_side)) for s in range(source_rows)
        ]

    def compare(block, column, group, upper, visit):
        line = weights_back[block * row_count + column, group * SUB : (group + 1) * SUB, :]
        for s in range(source_rows):
            visit(s, upper[s] + line == spread_at(lanes, column, group, s))

    for col_step in range(col_count):
        block = partner(my_col, col_step, col_count)
        if col_step:
            settle_upper(block)
        else:
            band[block] = lower[0, my_row]
        if keep_masks:

            def mark(column, carried, block=block):
                upper = upper_lines(block)
                for group in range(groups):

                    def keep(s, same, group=group):
                        masks[block * row_count + column, group, s] = jnp.where(same, 1.0, 0.0)

                    compare(block, column, group, upper, keep)
                return carried

            lax.fori_loop(0, row_count, mark, 0)

    def add_shares(block, column, total, upper):
        for group in range(groups):
            if keep_masks:
                for s in range(source_rows):
                    share = spread_at(lanes_more, column, group, s)
                    total[s] += masks[block * row_count + column, group, s] * share
            else:

                def add(s, same, group=group):
                    share = spread_at(lanes_more, column, group, s)
                    total[s] += jnp.where(same, share, 0.0)

                compare(block, column, group, upper, add)

    def coefficient(column, dependency):
        paths = lower[1, column]
        spread(
            jnp.where(paths > 0.5, (1.0 + dependency) / jnp.maximum(paths, 1.0), 0.0),
            lanes_more.at[column],
        )

    full_arrived(1, full_count)

    def lower_paths(chunk, carried):
        for t in range(row_chunk):
            column = chunk * row_chunk + t
            found = combine(
                [full_dist[g, column] for g in range(row_count)],
                [full_count[g, column] for g in range(row_count)],
            )
            is_source = source_mask((column * col_count + my_col) * tile_side)
            lower[1, column] = settle(*found, is_source)[1]
            coefficient(column, 0.0)
        return carried

    lax.fori_loop(0, row_count // row_chunk, lower_paths, 0)

    for col_step in reversed(range(col_count)):
        block = partner(my_col, col_step, col_count)

        def first_sums(column, total, block=block):
            total = list(total)
            add_shares(block, column, total, None if keep_masks else upper_lines(block))
            return tuple(total)

        total = lax.fori_loop(
            0,
            row_count,
            first_sums,
            tuple(jnp.zeros((SUB, tile_side), jnp.float32) for _ in range(source_rows)),
        )
        sums_out[0, block] = fold(list(total), jnp.add, sub)
        for row_step in reversed(range(row_count)):
            if row_step or col_step:
                other = partner(my_row, row_step, row_count)
                start(
                    sums_out.at[0, block],
                    sums_all.at[my_row, my_col],
                    all_send.at[LEVELS + 1, row_step, col_step],
                    all_recv.at[LEVELS + 1, my_row, my_col],
                    {"row": other, "col": block},
                )
            else:
                sums_all[my_row, my_col] = sums_out[0, block]

    packed[0] = jnp.where(lower[0, my_row] < half_far, lower[0, my_row], -1.0)
    packed[1] = lower[1, my_row]
    fill(col_count, 0.0)

    def from_columns(pair, carried):
        columns = [partner(my_row, pair * row_pair + t, row_count) for t in range(row_pair)]
        for t, column in enumerate(columns):
            for col_step in range(col_count):
                giver = partner(my_col, col_step, col_count)

                def wait(column=column, giver=giver):
                    arrived(
                        sums_all.at[column, giver],
                        all_recv.at[LEVELS + 1, column, giver],
                        {"row": column, "col": giver},
                    )

                if col_step == 0 and t == 0:
                    pl.when(pair > 0)(wait)
                else:
                    wait()
        for column in columns:
            summed = functools.reduce(jnp.add, [sums_all[column, g] for g in range(col_count)])
            coefficient(column, lower[1, column] * summed)

        def one_block(block, carried):
            total = [gathered[block, s] for s in range(source_rows)]
            upper = None if keep_masks else upper_lines(block)
            for column in columns:
                add_shares(block, column, total, upper)
            for s in range(source_rows):
                gathered[block, s] = total[s]
            return carried

        lax.fori_loop(0, col_count, one_block, 0)
        return carried

    lax.fori_loop(0, row_count // row_pair, from_columns, 0)

    for col_step in reversed(range(col_count)):
        block = partner(my_col, col_step, col_count)
        sums_out[1, block] = fold([gathered[block, s] for s in range(source_rows)], jnp.add, sub)
        if col_step:
            start(
                sums_out.at[1, block],
                sums_in.at[my_col],
                col_send.at[col_step],
                col_recv.at[my_col],
                {"row": my_row, "col": block},
            )
    summed = sums_out[1, my_col]
    for col_step in range(1, col_count):
        other = partner(my_col, col_step, col_count)
        arrived(sums_in.at[other], col_recv.at[other], {"row": my_row, "col": other})
        summed += sums_in[other]
    own_source = source_mask((my_row * col_count + my_col) * tile_side)
    packed[2] = jnp.where(own_source, 0.0, lower[1, my_row] * summed)
    for copy in pending:
        copy.wait_send()


def unpack(packed, dist_out, path_out, cent_out):
    dist_out[...] = packed[0]
    path_out[...] = packed[1]
    cent_out[...] = jnp.sum(packed[2], axis=0, keepdims=True) / packed.shape[1]


def solution(mesh):
    row_count = mesh.shape["row"]
    col_count = mesh.shape["col"]

    def per_device(tiles, tile_index, tile_count, sources):
        slot_total, tile_side = tiles.shape[0], tiles.shape[1]
        source_rows = sources.shape[0]
        wide = (source_rows, tile_side)
        positions = row_count * col_count
        longest = max(row_count, col_count)
        mask_shape = (positions, tile_side // SUB, source_rows, SUB, tile_side)
        if positions > MASK_TILES:
            mask_shape = (1, 1, 1, SUB, tile_side)
        vector = pl.BlockSpec(memory_space=pltpu.VMEM)
        packed = pl.pallas_call(
            functools.partial(body, row_count, col_count),
            out_shape=jax.ShapeDtypeStruct((3,) + wide, jnp.float32),
            in_specs=[pl.BlockSpec(memory_space=pl.ANY)] * 4,
            out_specs=vector,
            scratch_shapes=[
                pltpu.SMEM((2, slot_total), jnp.int32),
                pltpu.SMEM((1,), jnp.int32),
                pltpu.SMEM((source_rows,), jnp.int32),
                pltpu.VMEM((slot_total, tile_side, tile_side), jnp.float32),
                pltpu.SMEM((positions,), jnp.int32),
                pltpu.VMEM((positions, tile_side, tile_side), jnp.float32),
                pltpu.VMEM((positions, tile_side, tile_side), jnp.float32),
                pltpu.VMEM((4 * source_rows, source_rows * tile_side), jnp.bfloat16),
                pltpu.VMEM((longest, tile_side, source_rows * tile_side), jnp.float32),
                pltpu.VMEM((longest, tile_side, source_rows * tile_side), jnp.float32),
                pltpu.VMEM(mask_shape, jnp.float32),
                pltpu.VMEM((longest, source_rows, SUB, tile_side), jnp.float32),
                pltpu.VMEM((LEVELS, row_count) + wide, jnp.float32),
                pltpu.VMEM((LEVELS - 1, row_count) + wide, jnp.float32),
                pltpu.VMEM((LEVELS, col_count, row_count) + wide, jnp.float32),
                pltpu.VMEM((col_count, row_count) + wide, jnp.float32),
                pltpu.VMEM((row_count, row_count) + wide, jnp.float32),
                pltpu.VMEM((row_count, row_count) + wide, jnp.float32),
                pltpu.VMEM((col_count,) + wide, jnp.float32),
                pltpu.VMEM((2, row_count) + wide, jnp.float32),
                pltpu.VMEM((BACK, col_count) + wide, jnp.float32),
                pltpu.VMEM((row_count, col_count) + wide, jnp.float32),
                pltpu.VMEM((col_count,) + wide, jnp.float32),
                pltpu.SemaphoreType.DMA,
                pltpu.SemaphoreType.DMA((3,)),
                pltpu.SemaphoreType.DMA((LEVELS + 2, row_count, col_count)),
                pltpu.SemaphoreType.DMA((LEVELS + 2, row_count, col_count)),
                pltpu.SemaphoreType.DMA((2, row_count)),
                pltpu.SemaphoreType.DMA((2, row_count)),
                pltpu.SemaphoreType.DMA((col_count,)),
                pltpu.SemaphoreType.DMA((col_count,)),
            ],
            compiler_params=pltpu.CompilerParams(
                collective_id=0,
                has_side_effects=True,
            ),
        )(tile_index.T, tile_count, sources, tiles)
        distance, paths, centrality = pl.pallas_call(
            unpack,
            out_shape=(
                jax.ShapeDtypeStruct(wide, jnp.float32),
                jax.ShapeDtypeStruct(wide, jnp.float32),
                jax.ShapeDtypeStruct((1, tile_side), jnp.float32),
            ),
            in_specs=[vector],
            out_specs=(vector, vector, vector),
        )(packed)
        return distance, paths, centrality.reshape(tile_side)

    in_specs = (
        P(("groups", "row", "col"), None, None),
        P(("groups", "row", "col"), None),
        P(("groups", "row", "col")),
        P("groups"),
    )
    out_specs = (
        P("groups", ("row", "col")),
        P("groups", ("row", "col")),
        P(("groups", "row", "col")),
    )
    return jax.shard_map(
        per_device, mesh=mesh, in_specs=in_specs, out_specs=out_specs, check_vma=False
    )
```

```python
import functools

import jax
import jax.numpy as jnp
from jax import lax
from jax.experimental import pallas as pl
from jax.experimental.pallas import tpu as pltpu
from jax.sharding import PartitionSpec as P

LEVELS = 3
BACK = 2
CHUNK = 4
PAIR = 2
SUB = 8
MASK_TILES = 32

far_value = 1000000.0
no_edge = 2000000.0
half_far = 500000.0
scale_up = 2.0**60


def partner(me, step, count):
    if count & (count - 1):
        return (me + step) % count
    total = 0
    bit = 1
    while bit < count:
        total = total + ((me // bit) % 2 + (step // bit) % 2) % 2 * bit
        bit *= 2
    return total


def fold(parts, join, sub):
    half = SUB // 2
    while len(parts) > 1:
        low = sub % (2 * half) < half
        count = len(parts) // 2
        parts = [
            join(
                jnp.where(low, parts[k], parts[k + count]),
                pltpu.roll(jnp.where(low, parts[k + count], parts[k]), half, 0)
                if half * 2 == SUB
                else jnp.where(
                    low,
                    pltpu.roll(parts[k], SUB - half, 0),
                    pltpu.roll(parts[k + count], half, 0),
                ),
            )
            for k in range(count)
        ]
        half //= 2
    return parts[0]


def body(
    row_count,
    col_count,
    index_hbm,
    source_hbm,
    tiles_ref,
    packed,
    index_ref,
    source_ref,
    raw,
    place_ref,
    weights,
    weights_back,
    pick,
    lanes,
    lanes_even,
    lanes_odd,
    rows,
    masks,
    weighted,
    gathered,
    dist_out,
    count_out,
    dist_in,
    count_in,
    full_dist,
    full_count,
    band,
    lower,
    sums_out,
    sums_all,
    sums_in,
    load_sem,
    small_sem,
    all_send,
    all_recv,
    full_send,
    full_recv,
    col_send,
    col_recv,
):
    slot_total, tile_side = raw.shape[0], raw.shape[1]
    source_rows = source_ref.shape[0]
    my_row = lax.axis_index("row")
    my_col = lax.axis_index("col")
    positions = row_count * col_count
    row_chunk = CHUNK if row_count % CHUNK == 0 else 1
    col_chunk = CHUNK if col_count % CHUNK == 0 else 1
    row_pair = PAIR if row_count % PAIR == 0 else 1
    groups = tile_side // SUB
    wide = (source_rows, tile_side)
    last = LEVELS - 1
    keep_masks = masks.shape[0] > 1
    pending = []

    def others():
        for col_step in reversed(range(col_count)):
            for row_step in reversed(range(row_count)):
                if row_step or col_step:
                    yield (
                        partner(my_row, row_step, row_count),
                        partner(my_col, col_step, col_count),
                        row_step,
                        col_step,
                    )

    small = [
        pltpu.make_async_copy(index_hbm, index_ref, small_sem.at[0]),
        pltpu.make_async_copy(source_hbm, source_ref, small_sem.at[1]),
    ]
    for copy in small:
        copy.start()
    load = pltpu.make_async_copy(tiles_ref, raw, load_sem)
    load.start()
    barrier = pltpu.get_barrier_semaphore()
    for other_row, other_col, _, _ in others():
        pl.semaphore_signal(
            barrier,
            inc=1,
            device_id={"row": other_row, "col": other_col},
            device_id_type=pl.DeviceIdType.MESH,
        )

    def start(source, target, send, recv, device):
        copy = pltpu.make_async_remote_copy(
            src_ref=source,
            dst_ref=target,
            send_sem=send,
            recv_sem=recv,
            device_id=device,
            device_id_type=pl.DeviceIdType.MESH,
        )
        copy.start()
        pending.append(copy)

    def push_all(stage, source_of, target, with_own_col=True):
        for other_row, other_col, row_step, col_step in others():
            if col_step or with_own_col:
                start(
                    source_of(other_row, other_col),
                    target,
                    all_send.at[stage, row_step, col_step],
                    all_recv.at[stage, my_row, my_col],
                    {"row": other_row, "col": other_col},
                )

    def push_full(stage, source, target):
        target[my_row] = source[...]
        for row_step in reversed(range(1, row_count)):
            start(
                source,
                target.at[my_row],
                full_send.at[stage, row_step],
                full_recv.at[stage, my_row],
                {"row": partner(my_row, row_step, row_count), "col": my_col},
            )

    def arrived(target, recv, device):
        pltpu.make_async_remote_copy(
            src_ref=target,
            dst_ref=target,
            send_sem=load_sem,
            recv_sem=recv,
            device_id=device,
            device_id_type=pl.DeviceIdType.MESH,
        ).wait_recv()

    def full_arrived(stage, target):
        for row_step in range(1, row_count):
            other = partner(my_row, row_step, row_count)
            arrived(target.at[other], full_recv.at[stage, other], {"row": other, "col": my_col})

    def block_arrived(stage, target, block, own):
        for row_step in range(row_count):
            giver = partner(my_row, row_step, row_count)

            def wait():
                arrived(
                    target.at[block, giver],
                    all_recv.at[stage, giver, block],
                    {"row": giver, "col": block},
                )

            if row_step == 0 and own is not None:
                pl.when(jnp.logical_not(own))(wait)
            else:
                wait()

    def source_mask(base):
        wanted = jnp.full(wide, -1, jnp.int32)
        for row in range(source_rows):
            wanted = jnp.where(sub == row, source_ref[row] - base, wanted)
        return lane == wanted

    def settle(found_dist, found_count, is_source):
        start_dist = jnp.where(is_source, 0.0, far_value).astype(jnp.float32)
        settled = jnp.minimum(start_dist, found_dist)
        ones = jnp.where(is_source, 1.0, 0.0).astype(jnp.float32)
        return settled, ones + jnp.where(found_dist == settled, found_count, 0.0)

    def nearest(values):
        return functools.reduce(jnp.minimum, values)

    def combine(dists, counts):
        best = nearest(dists)
        total = functools.reduce(
            jnp.add, [jnp.where(d == best, n, 0.0) for d, n in zip(dists, counts, strict=True)]
        )
        return best, total

    def cut(value):
        high = value.astype(jnp.bfloat16).astype(jnp.float32)
        rest = value - high
        middle = rest.astype(jnp.bfloat16).astype(jnp.float32)
        return jnp.concatenate([high, middle, rest - middle, jnp.zeros_like(high)], axis=0)

    def spread(value, target):
        target[...] = lax.dot_general(
            cut(value * scale_up).astype(jnp.bfloat16),
            pick[...],
            (((0,), (0,)), ((), ())),
            preferred_element_type=jnp.float32,
        )

    def deal(value, target):
        pieces = cut(value)
        owner = lax.broadcasted_iota(jnp.int32, pieces.shape, 0) % source_rows
        for s in range(source_rows):
            target[:, s * tile_side : (s + 1) * tile_side] = jnp.where(
                owner == s, pieces, 0.0
            ).astype(jnp.bfloat16)

    def join(block):
        parts = [weighted[block, k * source_rows : (k + 1) * source_rows, :] for k in range(3)]
        return parts[0] + (parts[1] + parts[2])

    def add_weighted(columns, block):
        total = weighted[block]
        for column in columns:
            if keep_masks:
                total += jnp.dot(
                    rows[column], masks[block, column], preferred_element_type=jnp.float32
                )
            else:
                for s in range(source_rows):
                    total += jnp.dot(
                        rows[column, :, s * tile_side : (s + 1) * tile_side],
                        same_behind(block, column, s),
                        preferred_element_type=jnp.float32,
                    )
        weighted[block] = total

    def repeat(count, one):
        if count == 1:
            one(0)
        else:

            def step(place, carried):
                one(place)
                return carried

            lax.fori_loop(0, count, step, 0)

    def spread_at(ref, group, s):
        return ref[group * SUB : (group + 1) * SUB, s * tile_side : (s + 1) * tile_side]

    for copy in small:
        copy.wait()
    holds = [index_ref[0, slot] * row_count + index_ref[1, slot] for slot in range(slot_total)]

    def find_slot(position, carried):
        found = jnp.int32(-1)
        for slot in range(slot_total):
            found = jnp.where(holds[slot] == position, jnp.int32(slot), found)
        place_ref[position] = found
        return carried

    lax.fori_loop(0, positions, find_slot, 0)

    lane = lax.broadcasted_iota(jnp.int32, wide, 1)
    sub = lax.broadcasted_iota(jnp.int32, wide, 0)
    load.wait()

    band_base = my_row * col_count * tile_side

    part_row = lax.broadcasted_iota(jnp.int32, pick.shape, 0)
    part_source = lax.broadcasted_iota(jnp.int32, pick.shape, 1) // tile_side
    chosen = (part_row % source_rows == part_source) & (part_row < 3 * source_rows)
    pick[...] = jnp.where(chosen, 1.0 / scale_up, 0.0).astype(jnp.bfloat16)

    def first_level(column, carried):
        best = jnp.full(wide, far_value, jnp.float32)
        for row in range(source_rows):
            place = source_ref[row] - band_base
            inside = (place >= 0) & (place < col_count * tile_side)
            place = jnp.clip(place, 0, col_count * tile_side - 1)
            slot = place_ref[(place // tile_side) * row_count + column]
            line = raw[jnp.maximum(slot, 0), pl.ds(place % tile_side, 1), :]
            limit = jnp.where(inside & (slot >= 0), 0.0, far_value).astype(jnp.float32)
            best = jnp.where((sub == row) & (line > limit), line, best)
        dist_out[0, column] = best
        return carried

    lax.fori_loop(0, row_count, first_level, 0)
    dist_in[0, my_col, my_row] = dist_out[0, my_row]
    pl.semaphore_wait(barrier, row_count * col_count - 1)
    push_all(0, lambda other_row, other_col: dist_out.at[0, other_row], dist_in.at[0, my_col, my_row])

    def prepare(position, carried):
        slot = place_ref[position]
        tile = raw[jnp.maximum(slot, 0)]
        limit = jnp.where(slot >= 0, 0.0, far_value).astype(jnp.float32)
        weights[position] = jnp.where(tile > limit, tile, no_edge)
        return carried

    lax.fori_loop(0, positions, prepare, 0)

    def turn(position, carried):
        weights_back[position] = weights[position].T
        return carried

    lax.fori_loop(0, positions, turn, 0)

    def relax(block):
        def columns(chunk):
            first = chunk * row_chunk
            best = [[gathered[first + t, s] for s in range(source_rows)] for t in range(row_chunk)]
            for group in range(groups):
                lines = [
                    weights[block * row_count + first + t, group * SUB : (group + 1) * SUB, :]
                    for t in range(row_chunk)
                ]
                for s in range(source_rows):
                    near = spread_at(lanes.at[block], group, s)
                    for t in range(row_chunk):
                        best[t][s] = jnp.minimum(best[t][s], near + lines[t])
            for t in range(row_chunk):
                for s in range(source_rows):
                    gathered[first + t, s] = best[t][s]

        repeat(row_count // row_chunk, columns)

    def tally(level, block, shares):
        def columns(chunk):
            for first in range(0, row_chunk, row_pair):
                tally_pair(level, block, shares, chunk * row_chunk + first)

        repeat(row_count // row_chunk, columns)

    def tally_pair(level, block, shares, first):
        total = [[gathered[first + t, s] for s in range(source_rows)] for t in range(row_pair)]
        best = [
            [
                jnp.broadcast_to(dist_out[level, first + t, s : s + 1, :], (SUB, tile_side))
                for s in range(source_rows)
            ]
            for t in range(row_pair)
        ]
        for group in range(groups):
            lines = [
                weights[block * row_count + first + t, group * SUB : (group + 1) * SUB, :]
                for t in range(row_pair)
            ]
            for s in range(source_rows):
                near = spread_at(lanes.at[block], group, s)
                paths = 1.0 if shares is None else spread_at(shares, group, s)
                for t in range(row_pair):
                    total[t][s] += jnp.where(near + lines[t] == best[t][s], paths, 0.0)
        for t in range(row_pair):
            for s in range(source_rows):
                gathered[first + t, s] = total[t][s]

    def same_behind(block, column, s):
        below = lanes[column, :, s * tile_side : (s + 1) * tile_side]
        upper = band[block, s : s + 1, :]
        same = upper + weights_back[block * row_count + column] == below
        return jnp.where(same, 1.0, 0.0).astype(jnp.bfloat16)

    def fill(count, value):
        def one(place, carried):
            for s in range(source_rows):
                gathered[place, s] = jnp.full((SUB, tile_side), value, jnp.float32)
            return carried

        lax.fori_loop(0, count, one, 0)

    def block_source(block):
        return source_mask((my_row * col_count + block) * tile_side)

    def spread_dist(level, block):
        best = nearest([dist_in[level - 1, block, g] for g in range(row_count)])
        spread(jnp.where(block_source(block), 0.0, best), lanes.at[block])

    def wait_count(block, own):
        block_arrived(LEVELS, count_in, block, own)

    def spread_count(level, block, target):
        found = combine(
            [dist_in[level - 1, block, g] for g in range(row_count)],
            [count_in[block, g] for g in range(row_count)],
        )
        spread(settle(*found, block_source(block))[1], target)

    def forward(level):
        fill(row_count, far_value)
        final = partner(my_col, col_count - 1, col_count)

        def relax_block(step, carried):
            block = partner(my_col, step, col_count)
            block_arrived(level - 1, dist_in.at[level - 1], block, step == 0)
            spread_dist(level, block)
            relax(block)
            return carried

        lax.fori_loop(0, col_count - 1, relax_block, 0)
        block_arrived(level - 1, dist_in.at[level - 1], final, None if col_count > 1 else True)
        if level > 1:
            wait_count(my_col, True)
        spread_dist(level, final)
        if level > 1:
            spread_count(level, my_col, lanes_even)
        relax(final)

        def close_dist(column, carried):
            dist_out[level, column] = fold(
                [gathered[column, s] for s in range(source_rows)], jnp.minimum, sub
            )
            return carried

        lax.fori_loop(0, row_count, close_dist, 0)
        if level == last:
            push_full(0, dist_out.at[level], full_dist)
        else:
            dist_in[level, my_col, my_row] = dist_out[level, my_row]
        push_all(
            level,
            lambda other_row, other_col: dist_out.at[level, other_row],
            dist_in.at[level, my_col, my_row],
            level != last,
        )

        fill(row_count, 0.0)
        if level > 1:

            def tally_next(step, shares, following_shares):
                following = partner(my_col, step + 1, col_count)
                wait_count(following, None)
                spread_count(level, following, following_shares)
                tally(level, partner(my_col, step, col_count), shares)

            def tally_two(pair):
                tally_next(2 * pair, lanes_even, lanes_odd)
                tally_next(2 * pair + 1, lanes_odd, lanes_even)

            if col_count > 2:
                repeat((col_count - 1) // 2, tally_two)
            if col_count % 2:
                tally(level, final, lanes_even)
            else:
                tally_next(col_count - 2, lanes_even, lanes_odd)
                tally(level, final, lanes_odd)
        else:

            def tally_block(block, carried):
                tally(level, block, None)
                return carried

            lax.fori_loop(0, col_count, tally_block, 0)

        def close_count(column, carried):
            total = fold([gathered[column, s] for s in range(source_rows)], jnp.add, sub)
            if level == 1:
                total = jnp.where(dist_out[level, column] < half_far, total, 0.0)
            count_out[level - 1, column] = total
            return carried

        lax.fori_loop(0, row_count, close_count, 0)
        if level == last:
            push_full(1, count_out.at[level - 1], full_count)
        else:
            count_in[my_col, my_row] = count_out[level - 1, my_row]
            push_all(
                LEVELS,
                lambda other_row, other_col: count_out.at[level - 1, other_row],
                count_in.at[my_col, my_row],
            )

    for level in range(1, LEVELS):
        forward(level)

    full_arrived(0, full_dist)

    def lower_dist(chunk, carried):
        for t in range(row_chunk):
            column = chunk * row_chunk + t
            best = nearest([full_dist[g, column] for g in range(row_count)])
            is_source = source_mask((column * col_count + my_col) * tile_side)
            settled = jnp.where(is_source, 0.0, best)
            lower[0, column] = settled
            spread(settled, lanes.at[column])
        return carried

    lax.fori_loop(0, row_count // row_chunk, lower_dist, 0)

    def settle_upper(block):
        for row_step in range(row_count):
            giver = partner(my_row, row_step, row_count)
            arrived(
                dist_in.at[last, block, giver],
                all_recv.at[last, giver, block],
                {"row": giver, "col": block},
            )
        best = nearest([dist_in[last, block, g] for g in range(row_count)])
        is_source = source_mask((my_row * col_count + block) * tile_side)
        band[block] = jnp.where(is_source, 0.0, best)

    for col_step in range(col_count):
        block = partner(my_col, col_step, col_count)
        if col_step:
            settle_upper(block)
        else:
            band[block] = lower[0, my_row]
        if keep_masks:

            def keep(column, carried, block=block):
                for s in range(source_rows):
                    masks[block, column, s * tile_side : (s + 1) * tile_side, :] = same_behind(
                        block, column, s
                    )
                return carried

            lax.fori_loop(0, row_count, keep, 0)

    def coefficient(column, dependency):
        paths = lower[1, column]
        deal(
            jnp.where(paths > 0.5, (1.0 + dependency) / jnp.maximum(paths, 1.0), 0.0),
            rows.at[column],
        )

    full_arrived(1, full_count)

    def lower_paths(chunk, carried):
        for t in range(row_chunk):
            column = chunk * row_chunk + t
            found = combine(
                [full_dist[g, column] for g in range(row_count)],
                [full_count[g, column] for g in range(row_count)],
            )
            is_source = source_mask((column * col_count + my_col) * tile_side)
            lower[1, column] = settle(*found, is_source)[1]
            coefficient(column, 0.0)
        return carried

    lax.fori_loop(0, row_count // row_chunk, lower_paths, 0)

    weighted[...] = jnp.zeros_like(weighted)
    for col_step in reversed(range(col_count)):
        block = partner(my_col, col_step, col_count)

        def first_sums(chunk, block=block):
            add_weighted([chunk * row_chunk + t for t in range(row_chunk)], block)

        repeat(row_count // row_chunk, first_sums)
        sums_out[0, block] = join(block)
        for row_step in reversed(range(row_count)):
            if row_step or col_step:
                other = partner(my_row, row_step, row_count)
                start(
                    sums_out.at[0, block],
                    sums_all.at[my_row, my_col],
                    all_send.at[LEVELS + 1, row_step, col_step],
                    all_recv.at[LEVELS + 1, my_row, my_col],
                    {"row": other, "col": block},
                )
            else:
                sums_all[my_row, my_col] = sums_out[0, block]

    packed[0] = jnp.where(lower[0, my_row] < half_far, lower[0, my_row], -1.0)
    packed[1] = lower[1, my_row]
    weighted[...] = jnp.zeros_like(weighted)

    def from_columns(pair, carried):
        columns = [partner(my_row, pair * row_pair + t, row_count) for t in range(row_pair)]
        for t, column in enumerate(columns):
            for col_step in range(col_count):
                giver = partner(my_col, col_step, col_count)

                def wait(column=column, giver=giver):
                    arrived(
                        sums_all.at[column, giver],
                        all_recv.at[LEVELS + 1, column, giver],
                        {"row": column, "col": giver},
                    )

                if col_step == 0 and t == 0:
                    pl.when(pair > 0)(wait)
                else:
                    wait()
        for column in columns:
            summed = functools.reduce(jnp.add, [sums_all[column, g] for g in range(col_count)])
            coefficient(column, lower[1, column] * summed)

        def some_blocks(chunk):
            for t in range(col_chunk):
                add_weighted(columns, chunk * col_chunk + t)

        repeat(col_count // col_chunk, some_blocks)
        return carried

    lax.fori_loop(0, row_count // row_pair, from_columns, 0)

    early = len(pending)
    for col_step in reversed(range(col_count)):
        block = partner(my_col, col_step, col_count)
        sums_out[1, block] = join(block)
        if col_step:
            start(
                sums_out.at[1, block],
                sums_in.at[my_col],
                col_send.at[col_step],
                col_recv.at[my_col],
                {"row": my_row, "col": block},
            )
    for copy in pending[:early]:
        copy.wait_send()
    summed = sums_out[1, my_col]
    for col_step in range(1, col_count):
        other = partner(my_col, col_step, col_count)
        arrived(sums_in.at[other], col_recv.at[other], {"row": my_row, "col": other})
        summed += sums_in[other]
    own_source = source_mask((my_row * col_count + my_col) * tile_side)
    packed[2] = jnp.where(own_source, 0.0, lower[1, my_row] * summed)
    for copy in pending[early:]:
        copy.wait_send()


def unpack(packed, dist_out, path_out, cent_out):
    dist_out[...] = packed[0]
    path_out[...] = packed[1]
    cent_out[...] = jnp.sum(packed[2], axis=0, keepdims=True) / packed.shape[1]


def solution(mesh):
    row_count = mesh.shape["row"]
    col_count = mesh.shape["col"]

    def per_device(tiles, tile_index, tile_count, sources):
        del tile_count
        slot_total, tile_side = tiles.shape[0], tiles.shape[1]
        source_rows = sources.shape[0]
        wide = (source_rows, tile_side)
        positions = row_count * col_count
        longest = max(row_count, col_count)
        mask_shape = (col_count, row_count, source_rows * tile_side, tile_side)
        if positions > MASK_TILES:
            mask_shape = (1, 1, 2 * SUB, tile_side)
        vector = pl.BlockSpec(memory_space=pltpu.VMEM)
        packed = pl.pallas_call(
            functools.partial(body, row_count, col_count),
            out_shape=pltpu.VMEM((3,) + wide, jnp.float32),
            in_specs=[pl.BlockSpec(memory_space=pl.ANY)] * 3,
            out_specs=vector,
            scratch_shapes=[
                pltpu.SMEM((2, slot_total), jnp.int32),
                pltpu.SMEM((source_rows,), jnp.int32),
                pltpu.VMEM((slot_total, tile_side, tile_side), jnp.float32),
                pltpu.SMEM((positions,), jnp.int32),
                pltpu.VMEM((positions, tile_side, tile_side), jnp.float32),
                pltpu.VMEM((positions, tile_side, tile_side), jnp.float32),
                pltpu.VMEM((4 * source_rows, source_rows * tile_side), jnp.bfloat16),
                pltpu.VMEM((longest, tile_side, source_rows * tile_side), jnp.float32),
                pltpu.VMEM((tile_side, source_rows * tile_side), jnp.float32),
                pltpu.VMEM((tile_side, source_rows * tile_side), jnp.float32),
                pltpu.VMEM((longest, 4 * source_rows, source_rows * tile_side), jnp.bfloat16),
                pltpu.VMEM(mask_shape, jnp.bfloat16),
                pltpu.VMEM((col_count, 4 * source_rows, tile_side), jnp.float32),
                pltpu.VMEM((longest, source_rows, SUB, tile_side), jnp.float32),
                pltpu.VMEM((LEVELS, row_count) + wide, jnp.float32),
                pltpu.VMEM((LEVELS - 1, row_count) + wide, jnp.float32),
                pltpu.VMEM((LEVELS, col_count, row_count) + wide, jnp.float32),
                pltpu.VMEM((col_count, row_count) + wide, jnp.float32),
                pltpu.VMEM((row_count, row_count) + wide, jnp.float32),
                pltpu.VMEM((row_count, row_count) + wide, jnp.float32),
                pltpu.VMEM((col_count,) + wide, jnp.float32),
                pltpu.VMEM((2, row_count) + wide, jnp.float32),
                pltpu.VMEM((BACK, col_count) + wide, jnp.float32),
                pltpu.VMEM((row_count, col_count) + wide, jnp.float32),
                pltpu.VMEM((col_count,) + wide, jnp.float32),
                pltpu.SemaphoreType.DMA,
                pltpu.SemaphoreType.DMA((2,)),
                pltpu.SemaphoreType.DMA((LEVELS + 2, row_count, col_count)),
                pltpu.SemaphoreType.DMA((LEVELS + 2, row_count, col_count)),
                pltpu.SemaphoreType.DMA((2, row_count)),
                pltpu.SemaphoreType.DMA((2, row_count)),
                pltpu.SemaphoreType.DMA((col_count,)),
                pltpu.SemaphoreType.DMA((col_count,)),
            ],
            compiler_params=pltpu.CompilerParams(
                collective_id=0,
                has_side_effects=True,
            ),
        )(tile_index.T, sources, tiles)
        distance, paths, centrality = pl.pallas_call(
            unpack,
            out_shape=(
                jax.ShapeDtypeStruct(wide, jnp.float32),
                jax.ShapeDtypeStruct(wide, jnp.float32),
                jax.ShapeDtypeStruct((1, tile_side), jnp.float32),
            ),
            in_specs=[vector],
            out_specs=(vector, vector, vector),
            compiler_params=pltpu.CompilerParams(vmem_limit_bytes=2**20),
        )(packed)
        return distance, paths, centrality.reshape(tile_side)

    in_specs = (
        P(("groups", "row", "col"), None, None),
        P(("groups", "row", "col"), None),
        P(("groups", "row", "col")),
        P("groups"),
    )
    out_specs = (
        P("groups", ("row", "col")),
        P("groups", ("row", "col")),
        P(("groups", "row", "col")),
    )
    return jax.shard_map(
        per_device, mesh=mesh, in_specs=in_specs, out_specs=out_specs, check_vma=False
    )
```

```python
import functools

import jax
import jax.numpy as jnp
from jax import lax
from jax.experimental import pallas as pl
from jax.experimental.pallas import tpu as pltpu
from jax.sharding import PartitionSpec as P

LEVELS = 3
BACK = 2
CHUNK = 4
PAIR = 2
SUB = 8
MASK_TILES = 32

far_value = 1000000.0
no_edge = 2000000.0
half_far = 500000.0
scale_up = 2.0**60


def partner(me, step, count):
    if count & (count - 1):
        return (me + step) % count
    total = 0
    bit = 1
    while bit < count:
        total = total + ((me // bit) % 2 + (step // bit) % 2) % 2 * bit
        bit *= 2
    return total


def fold(parts, join, sub):
    half = SUB // 2
    while len(parts) > 1:
        low = sub % (2 * half) < half
        count = len(parts) // 2
        parts = [
            join(
                jnp.where(low, parts[k], parts[k + count]),
                pltpu.roll(jnp.where(low, parts[k + count], parts[k]), half, 0)
                if half * 2 == SUB
                else jnp.where(
                    low,
                    pltpu.roll(parts[k], SUB - half, 0),
                    pltpu.roll(parts[k + count], half, 0),
                ),
            )
            for k in range(count)
        ]
        half //= 2
    return parts[0]


def body(
    row_count,
    col_count,
    index_hbm,
    source_hbm,
    tiles_ref,
    packed,
    index_ref,
    source_ref,
    raw,
    place_ref,
    weights,
    weights_back,
    pick,
    lanes,
    lanes_even,
    lanes_odd,
    rows,
    masks,
    weighted,
    gathered,
    dist_out,
    count_out,
    dist_in,
    count_in,
    full_dist,
    full_count,
    band,
    lower,
    sums_out,
    sums_all,
    sums_in,
    load_sem,
    small_sem,
    all_send,
    all_recv,
    full_send,
    full_recv,
    col_send,
    col_recv,
):
    slot_total, tile_side = raw.shape[0], raw.shape[1]
    source_rows = source_ref.shape[0]
    my_row = lax.axis_index("row")
    my_col = lax.axis_index("col")
    positions = row_count * col_count
    row_chunk = CHUNK if row_count % CHUNK == 0 else 1
    col_chunk = CHUNK if col_count % CHUNK == 0 else 1
    row_pair = PAIR if row_count % PAIR == 0 else 1
    groups = tile_side // SUB
    wide = (source_rows, tile_side)
    last = LEVELS - 1
    keep_masks = masks.shape[0] > 1
    pending = []

    def others():
        for col_step in reversed(range(col_count)):
            for row_step in reversed(range(row_count)):
                if row_step or col_step:
                    yield (
                        partner(my_row, row_step, row_count),
                        partner(my_col, col_step, col_count),
                        row_step,
                        col_step,
                    )

    small = [
        pltpu.make_async_copy(index_hbm, index_ref, small_sem.at[0]),
        pltpu.make_async_copy(source_hbm, source_ref, small_sem.at[1]),
    ]
    for copy in small:
        copy.start()
    load = pltpu.make_async_copy(tiles_ref, raw, load_sem)
    load.start()
    barrier = pltpu.get_barrier_semaphore()
    for other_row, other_col, _, _ in others():
        pl.semaphore_signal(
            barrier,
            inc=1,
            device_id={"row": other_row, "col": other_col},
            device_id_type=pl.DeviceIdType.MESH,
        )

    def start(source, target, send, recv, device):
        copy = pltpu.make_async_remote_copy(
            src_ref=source,
            dst_ref=target,
            send_sem=send,
            recv_sem=recv,
            device_id=device,
            device_id_type=pl.DeviceIdType.MESH,
        )
        copy.start()
        pending.append(copy)

    def push_all(stage, source_of, target):
        for other_row, other_col, row_step, col_step in others():
            start(
                source_of(other_row, other_col),
                target,
                all_send.at[stage, row_step, col_step],
                all_recv.at[stage, my_row, my_col],
                {"row": other_row, "col": other_col},
            )

    def push_full(stage, source, target):
        target[my_row] = source[...]
        for row_step in reversed(range(1, row_count)):
            start(
                source,
                target.at[my_row],
                full_send.at[stage, row_step],
                full_recv.at[stage, my_row],
                {"row": partner(my_row, row_step, row_count), "col": my_col},
            )

    def arrived(target, recv, device):
        pltpu.make_async_remote_copy(
            src_ref=target,
            dst_ref=target,
            send_sem=load_sem,
            recv_sem=recv,
            device_id=device,
            device_id_type=pl.DeviceIdType.MESH,
        ).wait_recv()

    def full_arrived(stage, target):
        for row_step in range(1, row_count):
            other = partner(my_row, row_step, row_count)
            arrived(target.at[other], full_recv.at[stage, other], {"row": other, "col": my_col})

    def block_arrived(stage, target, block, own):
        for row_step in range(row_count):
            giver = partner(my_row, row_step, row_count)

            def wait():
                arrived(
                    target.at[block, giver],
                    all_recv.at[stage, giver, block],
                    {"row": giver, "col": block},
                )

            if row_step == 0 and own is not None:
                pl.when(jnp.logical_not(own))(wait)
            else:
                wait()

    def source_mask(base):
        wanted = jnp.full(wide, -1, jnp.int32)
        for row in range(source_rows):
            wanted = jnp.where(sub == row, source_ref[row] - base, wanted)
        return lane == wanted

    def settle(found_dist, found_count, is_source):
        start_dist = jnp.where(is_source, 0.0, far_value).astype(jnp.float32)
        settled = jnp.minimum(start_dist, found_dist)
        ones = jnp.where(is_source, 1.0, 0.0).astype(jnp.float32)
        return settled, ones + jnp.where(found_dist == settled, found_count, 0.0)

    def nearest(values):
        return functools.reduce(jnp.minimum, values)

    def combine(dists, counts):
        best = nearest(dists)
        total = functools.reduce(
            jnp.add, [jnp.where(d == best, n, 0.0) for d, n in zip(dists, counts, strict=True)]
        )
        return best, total

    def cut(value):
        high = value.astype(jnp.bfloat16).astype(jnp.float32)
        rest = value - high
        middle = rest.astype(jnp.bfloat16).astype(jnp.float32)
        return jnp.concatenate([high, middle, rest - middle, jnp.zeros_like(high)], axis=0)

    def spread(value, target):
        target[...] = lax.dot_general(
            cut(value * scale_up).astype(jnp.bfloat16),
            pick[...],
            (((0,), (0,)), ((), ())),
            preferred_element_type=jnp.float32,
        )

    def deal(value, target):
        pieces = cut(value)
        owner = lax.broadcasted_iota(jnp.int32, pieces.shape, 0) % source_rows
        for s in range(source_rows):
            target[:, s * tile_side : (s + 1) * tile_side] = jnp.where(
                owner == s, pieces, 0.0
            ).astype(jnp.bfloat16)

    def join(block):
        parts = [weighted[block, k * source_rows : (k + 1) * source_rows, :] for k in range(3)]
        return parts[0] + (parts[1] + parts[2])

    def add_weighted(columns, block):
        total = weighted[block]
        for column in columns:
            if keep_masks:
                total += jnp.dot(
                    rows[column], masks[block, column], preferred_element_type=jnp.float32
                )
            else:
                for s in range(source_rows):
                    total += jnp.dot(
                        rows[column, :, s * tile_side : (s + 1) * tile_side],
                        same_behind(block, column, s),
                        preferred_element_type=jnp.float32,
                    )
        weighted[block] = total

    def repeat(count, one):
        if count == 1:
            one(0)
        else:

            def step(place, carried):
                one(place)
                return carried

            lax.fori_loop(0, count, step, 0)

    def spread_at(ref, group, s):
        return ref[group * SUB : (group + 1) * SUB, s * tile_side : (s + 1) * tile_side]

    for copy in small:
        copy.wait()
    holds = [index_ref[0, slot] * row_count + index_ref[1, slot] for slot in range(slot_total)]

    def find_slot(position, carried):
        found = jnp.int32(-1)
        for slot in range(slot_total):
            found = jnp.where(holds[slot] == position, jnp.int32(slot), found)
        place_ref[position] = found
        return carried

    lax.fori_loop(0, positions, find_slot, 0)

    lane = lax.broadcasted_iota(jnp.int32, wide, 1)
    sub = lax.broadcasted_iota(jnp.int32, wide, 0)
    load.wait()

    band_base = my_row * col_count * tile_side

    part_row = lax.broadcasted_iota(jnp.int32, pick.shape, 0)
    part_source = lax.broadcasted_iota(jnp.int32, pick.shape, 1) // tile_side
    chosen = (part_row % source_rows == part_source) & (part_row < 3 * source_rows)
    pick[...] = jnp.where(chosen, 1.0 / scale_up, 0.0).astype(jnp.bfloat16)

    def first_level(column, carried):
        best = jnp.full(wide, far_value, jnp.float32)
        for row in range(source_rows):
            place = source_ref[row] - band_base
            inside = (place >= 0) & (place < col_count * tile_side)
            place = jnp.clip(place, 0, col_count * tile_side - 1)
            slot = place_ref[(place // tile_side) * row_count + column]
            line = raw[jnp.maximum(slot, 0), pl.ds(place % tile_side, 1), :]
            limit = jnp.where(inside & (slot >= 0), 0.0, far_value).astype(jnp.float32)
            best = jnp.where((sub == row) & (line > limit), line, best)
        dist_out[0, column] = best
        return carried

    lax.fori_loop(0, row_count, first_level, 0)
    dist_in[0, my_col, my_row] = dist_out[0, my_row]
    pl.semaphore_wait(barrier, row_count * col_count - 1)
    push_all(0, lambda other_row, other_col: dist_out.at[0, other_row], dist_in.at[0, my_col, my_row])

    def prepare(position, carried):
        slot = place_ref[position]
        tile = raw[jnp.maximum(slot, 0)]
        limit = jnp.where(slot >= 0, 0.0, far_value).astype(jnp.float32)
        weights[position] = jnp.where(tile > limit, tile, no_edge)
        return carried

    lax.fori_loop(0, positions, prepare, 0)

    def turn(position, carried):
        weights_back[position] = weights[position].T
        return carried

    lax.fori_loop(0, positions, turn, 0)

    def relax(block):
        near = lanes.at[block]

        def columns(chunk):
            first = chunk * row_chunk
            for s in range(source_rows):
                best = [gathered[first + t, s] for t in range(row_chunk)]
                for group in range(groups):
                    value = spread_at(near, group, s)
                    for t in range(row_chunk):
                        line = weights[
                            block * row_count + first + t, group * SUB : (group + 1) * SUB, :
                        ]
                        best[t] = jnp.minimum(best[t], value + line)
                for t in range(row_chunk):
                    gathered[first + t, s] = best[t]

        repeat(row_count // row_chunk, columns)

    def relax_column(level, block, column):
        near = lanes.at[block]
        best = [gathered[column, s] for s in range(source_rows)]
        for group in range(groups):
            line = weights[block * row_count + column, group * SUB : (group + 1) * SUB, :]
            for s in range(source_rows):
                best[s] = jnp.minimum(best[s], spread_at(near, group, s) + line)
        dist_out[level, column] = fold(best, jnp.minimum, sub)

    def tally(level, block, shares):
        def columns(chunk):
            for first in range(0, row_chunk, row_pair):
                tally_pair(level, block, shares, chunk * row_chunk + first)

        repeat(row_count // row_chunk, columns)

    def tally_pair(level, block, shares, first):
        total = [[gathered[first + t, s] for s in range(source_rows)] for t in range(row_pair)]
        best = [
            [
                jnp.broadcast_to(dist_out[level, first + t, s : s + 1, :], (SUB, tile_side))
                for s in range(source_rows)
            ]
            for t in range(row_pair)
        ]
        for group in range(groups):
            lines = [
                weights[block * row_count + first + t, group * SUB : (group + 1) * SUB, :]
                for t in range(row_pair)
            ]
            for s in range(source_rows):
                near = spread_at(lanes.at[block], group, s)
                paths = 1.0 if shares is None else spread_at(shares, group, s)
                for t in range(row_pair):
                    total[t][s] += jnp.where(near + lines[t] == best[t][s], paths, 0.0)
        for t in range(row_pair):
            for s in range(source_rows):
                gathered[first + t, s] = total[t][s]

    def same_behind(block, column, s):
        below = lanes[column, :, s * tile_side : (s + 1) * tile_side]
        upper = band[block, s : s + 1, :]
        same = upper + weights_back[block * row_count + column] == below
        return jnp.where(same, 1.0, 0.0).astype(jnp.bfloat16)

    def fill(count, value):
        def one(place, carried):
            for s in range(source_rows):
                gathered[place, s] = jnp.full((SUB, tile_side), value, jnp.float32)
            return carried

        lax.fori_loop(0, count, one, 0)

    def block_source(block):
        return source_mask((my_row * col_count + block) * tile_side)

    def spread_dist(level, block):
        best = nearest([dist_in[level - 1, block, g] for g in range(row_count)])
        spread(jnp.where(block_source(block), 0.0, best), lanes.at[block])

    def wait_count(block, own):
        block_arrived(LEVELS, count_in, block, own)

    def spread_count(level, block, target):
        found = combine(
            [dist_in[level - 1, block, g] for g in range(row_count)],
            [count_in[block, g] for g in range(row_count)],
        )
        spread(settle(*found, block_source(block))[1], target)

    def forward(level):
        fill(row_count, far_value)
        final = partner(my_col, col_count - 1, col_count)

        def relax_block(step, carried):
            block = partner(my_col, step, col_count)
            block_arrived(level - 1, dist_in.at[level - 1], block, step == 0)
            spread_dist(level, block)
            relax(block)
            return carried

        lax.fori_loop(0, col_count - 1, relax_block, 0)
        block_arrived(level - 1, dist_in.at[level - 1], final, None if col_count > 1 else True)
        if level > 1:
            wait_count(my_col, True)
        spread_dist(level, final)
        if level > 1:
            spread_count(level, my_col, lanes_even)
        for row_step in reversed(range(row_count)):
            column = partner(my_row, row_step, row_count)
            relax_column(level, final, column)
            for col_step in reversed(range(col_count)):
                if (row_step or col_step) and (col_step or level != last):
                    start(
                        dist_out.at[level, column],
                        dist_in.at[level, my_col, my_row],
                        all_send.at[level, row_step, col_step],
                        all_recv.at[level, my_row, my_col],
                        {"row": column, "col": partner(my_col, col_step, col_count)},
                    )
        if level == last:
            push_full(0, dist_out.at[level], full_dist)
        else:
            dist_in[level, my_col, my_row] = dist_out[level, my_row]

        fill(row_count, 0.0)
        if level > 1:

            def tally_next(step, shares, following_shares):
                following = partner(my_col, step + 1, col_count)
                wait_count(following, None)
                tally(level, partner(my_col, step, col_count), shares)
                spread_count(level, following, following_shares)

            def tally_two(pair):
                tally_next(2 * pair, lanes_even, lanes_odd)
                tally_next(2 * pair + 1, lanes_odd, lanes_even)

            if col_count > 2:
                repeat((col_count - 1) // 2, tally_two)
            if col_count % 2:
                tally(level, final, lanes_even)
            else:
                tally_next(col_count - 2, lanes_even, lanes_odd)
                tally(level, final, lanes_odd)
        else:

            def tally_block(block, carried):
                tally(level, block, None)
                return carried

            lax.fori_loop(0, col_count, tally_block, 0)

        def close_count(column, carried):
            total = fold([gathered[column, s] for s in range(source_rows)], jnp.add, sub)
            if level == 1:
                total = jnp.where(dist_out[level, column] < half_far, total, 0.0)
            count_out[level - 1, column] = total
            return carried

        lax.fori_loop(0, row_count, close_count, 0)
        if level == last:
            push_full(1, count_out.at[level - 1], full_count)
        else:
            count_in[my_col, my_row] = count_out[level - 1, my_row]
            push_all(
                LEVELS,
                lambda other_row, other_col: count_out.at[level - 1, other_row],
                count_in.at[my_col, my_row],
            )

    for level in range(1, LEVELS):
        forward(level)

    full_arrived(0, full_dist)

    def lower_dist(chunk, carried):
        for t in range(row_chunk):
            column = chunk * row_chunk + t
            best = nearest([full_dist[g, column] for g in range(row_count)])
            is_source = source_mask((column * col_count + my_col) * tile_side)
            settled = jnp.where(is_source, 0.0, best)
            lower[0, column] = settled
            spread(settled, lanes.at[column])
        return carried

    lax.fori_loop(0, row_count // row_chunk, lower_dist, 0)

    def settle_upper(block):
        for row_step in range(row_count):
            giver = partner(my_row, row_step, row_count)
            arrived(
                dist_in.at[last, block, giver],
                all_recv.at[last, giver, block],
                {"row": giver, "col": block},
            )
        best = nearest([dist_in[last, block, g] for g in range(row_count)])
        is_source = source_mask((my_row * col_count + block) * tile_side)
        band[block] = jnp.where(is_source, 0.0, best)

    for col_step in range(col_count):
        block = partner(my_col, col_step, col_count)
        if col_step:
            settle_upper(block)
        else:
            band[block] = lower[0, my_row]
        if keep_masks:

            def keep(column, carried, block=block):
                for s in range(source_rows):
                    masks[block, column, s * tile_side : (s + 1) * tile_side, :] = same_behind(
                        block, column, s
                    )
                return carried

            lax.fori_loop(0, row_count, keep, 0)

    def coefficient(column, dependency):
        paths = lower[1, column]
        deal(
            jnp.where(paths > 0.5, (1.0 + dependency) / jnp.maximum(paths, 1.0), 0.0),
            rows.at[column],
        )

    full_arrived(1, full_count)

    def lower_paths(chunk, carried):
        for t in range(row_chunk):
            column = chunk * row_chunk + t
            found = combine(
                [full_dist[g, column] for g in range(row_count)],
                [full_count[g, column] for g in range(row_count)],
            )
            is_source = source_mask((column * col_count + my_col) * tile_side)
            lower[1, column] = settle(*found, is_source)[1]
            coefficient(column, 0.0)
        return carried

    lax.fori_loop(0, row_count // row_chunk, lower_paths, 0)

    weighted[...] = jnp.zeros_like(weighted)
    for col_step in reversed(range(col_count)):
        block = partner(my_col, col_step, col_count)

        def first_sums(chunk, block=block):
            add_weighted([chunk * row_chunk + t for t in range(row_chunk)], block)

        repeat(row_count // row_chunk, first_sums)
        sums_out[0, block] = join(block)
        for row_step in reversed(range(row_count)):
            if row_step or col_step:
                other = partner(my_row, row_step, row_count)
                start(
                    sums_out.at[0, block],
                    sums_all.at[my_row, my_col],
                    all_send.at[LEVELS + 1, row_step, col_step],
                    all_recv.at[LEVELS + 1, my_row, my_col],
                    {"row": other, "col": block},
                )
            else:
                sums_all[my_row, my_col] = sums_out[0, block]

    packed[0] = jnp.where(lower[0, my_row] < half_far, lower[0, my_row], -1.0)
    packed[1] = lower[1, my_row]
    weighted[...] = jnp.zeros_like(weighted)

    def settle_columns(pair, own):
        columns = [partner(my_row, pair * row_pair + t, row_count) for t in range(row_pair)]
        for t, column in enumerate(columns):
            for col_step in range(col_count):
                giver = partner(my_col, col_step, col_count)

                def wait(column=column, giver=giver):
                    arrived(
                        sums_all.at[column, giver],
                        all_recv.at[LEVELS + 1, column, giver],
                        {"row": column, "col": giver},
                    )

                if col_step == 0 and t == 0 and own is not None:
                    pl.when(jnp.logical_not(own))(wait)
                else:
                    wait()
        for column in columns:
            summed = functools.reduce(jnp.add, [sums_all[column, g] for g in range(col_count)])
            coefficient(column, lower[1, column] * summed)
        return columns

    def from_columns(pair, carried):
        columns = settle_columns(pair, pair == 0)

        def some_blocks(chunk):
            for t in range(col_chunk):
                add_weighted(columns, chunk * col_chunk + t)

        repeat(col_count // col_chunk, some_blocks)
        return carried

    pairs = row_count // row_pair
    lax.fori_loop(0, pairs - 1, from_columns, 0)
    columns = settle_columns(pairs - 1, None if pairs > 1 else True)
    early = len(pending)
    for col_step in reversed(range(col_count)):
        block = partner(my_col, col_step, col_count)
        add_weighted(columns, block)
        sums_out[1, block] = join(block)
        if col_step:
            start(
                sums_out.at[1, block],
                sums_in.at[my_col],
                col_send.at[col_step],
                col_recv.at[my_col],
                {"row": my_row, "col": block},
            )
    for copy in pending[:early]:
        copy.wait_send()
    summed = sums_out[1, my_col]
    for col_step in range(1, col_count):
        other = partner(my_col, col_step, col_count)
        arrived(sums_in.at[other], col_recv.at[other], {"row": my_row, "col": other})
        summed += sums_in[other]
    own_source = source_mask((my_row * col_count + my_col) * tile_side)
    packed[2] = jnp.where(own_source, 0.0, lower[1, my_row] * summed)
    for copy in pending[early:]:
        copy.wait_send()


def unpack(packed, dist_out, path_out, cent_out):
    dist_out[...] = packed[0]
    path_out[...] = packed[1]
    cent_out[...] = jnp.sum(packed[2], axis=0, keepdims=True) / packed.shape[1]


def solution(mesh):
    row_count = mesh.shape["row"]
    col_count = mesh.shape["col"]

    def per_device(tiles, tile_index, tile_count, sources):
        del tile_count
        slot_total, tile_side = tiles.shape[0], tiles.shape[1]
        source_rows = sources.shape[0]
        wide = (source_rows, tile_side)
        positions = row_count * col_count
        longest = max(row_count, col_count)
        mask_shape = (col_count, row_count, source_rows * tile_side, tile_side)
        if positions > MASK_TILES:
            mask_shape = (1, 1, 2 * SUB, tile_side)
        vector = pl.BlockSpec(memory_space=pltpu.VMEM)
        packed = pl.pallas_call(
            functools.partial(body, row_count, col_count),
            out_shape=pltpu.VMEM((3,) + wide, jnp.float32),
            in_specs=[pl.BlockSpec(memory_space=pl.ANY)] * 3,
            out_specs=vector,
            scratch_shapes=[
                pltpu.SMEM((2, slot_total), jnp.int32),
                pltpu.SMEM((source_rows,), jnp.int32),
                pltpu.VMEM((slot_total, tile_side, tile_side), jnp.float32),
                pltpu.SMEM((positions,), jnp.int32),
                pltpu.VMEM((positions, tile_side, tile_side), jnp.float32),
                pltpu.VMEM((positions, tile_side, tile_side), jnp.float32),
                pltpu.VMEM((4 * source_rows, source_rows * tile_side), jnp.bfloat16),
                pltpu.VMEM((longest, tile_side, source_rows * tile_side), jnp.float32),
                pltpu.VMEM((tile_side, source_rows * tile_side), jnp.float32),
                pltpu.VMEM((tile_side, source_rows * tile_side), jnp.float32),
                pltpu.VMEM((longest, 4 * source_rows, source_rows * tile_side), jnp.bfloat16),
                pltpu.VMEM(mask_shape, jnp.bfloat16),
                pltpu.VMEM((col_count, 4 * source_rows, tile_side), jnp.float32),
                pltpu.VMEM((longest, source_rows, SUB, tile_side), jnp.float32),
                pltpu.VMEM((LEVELS, row_count) + wide, jnp.float32),
                pltpu.VMEM((LEVELS - 1, row_count) + wide, jnp.float32),
                pltpu.VMEM((LEVELS, col_count, row_count) + wide, jnp.float32),
                pltpu.VMEM((col_count, row_count) + wide, jnp.float32),
                pltpu.VMEM((row_count, row_count) + wide, jnp.float32),
                pltpu.VMEM((row_count, row_count) + wide, jnp.float32),
                pltpu.VMEM((col_count,) + wide, jnp.float32),
                pltpu.VMEM((2, row_count) + wide, jnp.float32),
                pltpu.VMEM((BACK, col_count) + wide, jnp.float32),
                pltpu.VMEM((row_count, col_count) + wide, jnp.float32),
                pltpu.VMEM((col_count,) + wide, jnp.float32),
                pltpu.SemaphoreType.DMA,
                pltpu.SemaphoreType.DMA((2,)),
                pltpu.SemaphoreType.DMA((LEVELS + 2, row_count, col_count)),
                pltpu.SemaphoreType.DMA((LEVELS + 2, row_count, col_count)),
                pltpu.SemaphoreType.DMA((2, row_count)),
                pltpu.SemaphoreType.DMA((2, row_count)),
                pltpu.SemaphoreType.DMA((col_count,)),
                pltpu.SemaphoreType.DMA((col_count,)),
            ],
            compiler_params=pltpu.CompilerParams(
                collective_id=0,
                has_side_effects=True,
            ),
        )(tile_index.T, sources, tiles)
        distance, paths, centrality = pl.pallas_call(
            unpack,
            out_shape=(
                jax.ShapeDtypeStruct(wide, jnp.float32),
                jax.ShapeDtypeStruct(wide, jnp.float32),
                jax.ShapeDtypeStruct((1, tile_side), jnp.float32),
            ),
            in_specs=[vector],
            out_specs=(vector, vector, vector),
            compiler_params=pltpu.CompilerParams(vmem_limit_bytes=2**20),
        )(packed)
        return distance, paths, centrality.reshape(tile_side)

    in_specs = (
        P(("groups", "row", "col"), None, None),
        P(("groups", "row", "col"), None),
        P(("groups", "row", "col")),
        P("groups"),
    )
    out_specs = (
        P("groups", ("row", "col")),
        P("groups", ("row", "col")),
        P(("groups", "row", "col")),
    )
    return jax.shard_map(
        per_device, mesh=mesh, in_specs=in_specs, out_specs=out_specs, check_vma=False
    )
```

```python
import functools

import jax
import jax.numpy as jnp
from jax import lax
from jax.experimental import pallas as pl
from jax.experimental.pallas import tpu as pltpu
from jax.sharding import PartitionSpec as P

LEVELS = 3
BACK = 2
CHUNK = 4
PAIR = 2
SUB = 8
MASK_TILES = 32

far_value = 1000000.0
no_edge = 2000000.0
half_far = 500000.0
scale_up = 2.0**60


def partner(me, step, count):
    if count & (count - 1):
        return (me + step) % count
    total = 0
    bit = 1
    while bit < count:
        total = total + ((me // bit) % 2 + (step // bit) % 2) % 2 * bit
        bit *= 2
    return total


def fold(parts, join, sub):
    half = SUB // 2
    while len(parts) > 1:
        low = sub % (2 * half) < half
        count = len(parts) // 2
        parts = [
            join(
                jnp.where(low, parts[k], parts[k + count]),
                pltpu.roll(jnp.where(low, parts[k + count], parts[k]), half, 0)
                if half * 2 == SUB
                else jnp.where(
                    low,
                    pltpu.roll(parts[k], SUB - half, 0),
                    pltpu.roll(parts[k + count], half, 0),
                ),
            )
            for k in range(count)
        ]
        half //= 2
    return parts[0]


def body(
    row_count,
    col_count,
    index_hbm,
    source_hbm,
    tiles_ref,
    packed,
    index_ref,
    source_ref,
    raw,
    place_ref,
    weights,
    weights_back,
    pick,
    lanes,
    lanes_even,
    lanes_odd,
    rows,
    masks,
    weighted,
    gathered,
    dist_out,
    count_out,
    dist_in,
    count_in,
    full_dist,
    full_count,
    band,
    lower,
    sums_out,
    sums_all,
    sums_in,
    load_sem,
    small_sem,
    all_send,
    all_recv,
    full_send,
    full_recv,
    col_send,
    col_recv,
):
    slot_total, tile_side = raw.shape[0], raw.shape[1]
    source_rows = source_ref.shape[0]
    my_row = lax.axis_index("row")
    my_col = lax.axis_index("col")
    positions = row_count * col_count
    row_chunk = CHUNK if row_count % CHUNK == 0 else 1
    col_chunk = CHUNK if col_count % CHUNK == 0 else 1
    row_pair = PAIR if row_count % PAIR == 0 else 1
    groups = tile_side // SUB
    wide = (source_rows, tile_side)
    last = LEVELS - 1
    keep_masks = masks.shape[0] > 1
    pending = []

    def others():
        for col_step in reversed(range(col_count)):
            for row_step in reversed(range(row_count)):
                if row_step or col_step:
                    yield (
                        partner(my_row, row_step, row_count),
                        partner(my_col, col_step, col_count),
                        row_step,
                        col_step,
                    )

    small = [
        pltpu.make_async_copy(index_hbm, index_ref, small_sem.at[0]),
        pltpu.make_async_copy(source_hbm, source_ref, small_sem.at[1]),
    ]
    for copy in small:
        copy.start()
    load = pltpu.make_async_copy(tiles_ref, raw, load_sem)
    load.start()
    barrier = pltpu.get_barrier_semaphore()
    for other_row, other_col, _, _ in others():
        pl.semaphore_signal(
            barrier,
            inc=1,
            device_id={"row": other_row, "col": other_col},
            device_id_type=pl.DeviceIdType.MESH,
        )

    def start(source, target, send, recv, device):
        copy = pltpu.make_async_remote_copy(
            src_ref=source,
            dst_ref=target,
            send_sem=send,
            recv_sem=recv,
            device_id=device,
            device_id_type=pl.DeviceIdType.MESH,
        )
        copy.start()
        pending.append(copy)

    def push_all(stage, source_of, target):
        for other_row, other_col, row_step, col_step in others():
            start(
                source_of(other_row, other_col),
                target,
                all_send.at[stage, row_step, col_step],
                all_recv.at[stage, my_row, my_col],
                {"row": other_row, "col": other_col},
            )

    def push_full(stage, source, target):
        target[my_row] = source[...]
        for row_step in reversed(range(1, row_count)):
            start(
                source,
                target.at[my_row],
                full_send.at[stage, row_step],
                full_recv.at[stage, my_row],
                {"row": partner(my_row, row_step, row_count), "col": my_col},
            )

    def arrived(target, recv, device):
        pltpu.make_async_remote_copy(
            src_ref=target,
            dst_ref=target,
            send_sem=load_sem,
            recv_sem=recv,
            device_id=device,
            device_id_type=pl.DeviceIdType.MESH,
        ).wait_recv()

    def full_arrived(stage, target):
        for row_step in range(1, row_count):
            other = partner(my_row, row_step, row_count)
            arrived(target.at[other], full_recv.at[stage, other], {"row": other, "col": my_col})

    def block_arrived(stage, target, block, own):
        for row_step in range(row_count):
            giver = partner(my_row, row_step, row_count)

            def wait():
                arrived(
                    target.at[block, giver],
                    all_recv.at[stage, giver, block],
                    {"row": giver, "col": block},
                )

            if row_step == 0 and own is not None:
                pl.when(jnp.logical_not(own))(wait)
            else:
                wait()

    def source_mask(base):
        wanted = jnp.full(wide, -1, jnp.int32)
        for row in range(source_rows):
            wanted = jnp.where(sub == row, source_ref[row] - base, wanted)
        return lane == wanted

    def settle(found_dist, found_count, is_source):
        start_dist = jnp.where(is_source, 0.0, far_value).astype(jnp.float32)
        settled = jnp.minimum(start_dist, found_dist)
        ones = jnp.where(is_source, 1.0, 0.0).astype(jnp.float32)
        return settled, ones + jnp.where(found_dist == settled, found_count, 0.0)

    def nearest(values):
        return functools.reduce(jnp.minimum, values)

    def combine(dists, counts):
        best = nearest(dists)
        total = functools.reduce(
            jnp.add, [jnp.where(d == best, n, 0.0) for d, n in zip(dists, counts, strict=True)]
        )
        return best, total

    def cut(value):
        high = value.astype(jnp.bfloat16).astype(jnp.float32)
        rest = value - high
        middle = rest.astype(jnp.bfloat16).astype(jnp.float32)
        return jnp.concatenate([high, middle, rest - middle, jnp.zeros_like(high)], axis=0)

    def spread(value, target):
        target[...] = lax.dot_general(
            cut(value * scale_up).astype(jnp.bfloat16),
            pick[...],
            (((0,), (0,)), ((), ())),
            preferred_element_type=jnp.float32,
        )

    def deal(value, target):
        pieces = cut(value)
        owner = lax.broadcasted_iota(jnp.int32, pieces.shape, 0) % source_rows
        for s in range(source_rows):
            target[:, s * tile_side : (s + 1) * tile_side] = jnp.where(
                owner == s, pieces, 0.0
            ).astype(jnp.bfloat16)

    def join(block):
        parts = [weighted[block, k * source_rows : (k + 1) * source_rows, :] for k in range(3)]
        return parts[0] + (parts[1] + parts[2])

    def add_weighted(columns, block):
        total = weighted[block]
        for column in columns:
            if keep_masks:
                total += jnp.dot(
                    rows[column], masks[block, column], preferred_element_type=jnp.float32
                )
            else:
                for s in range(source_rows):
                    total += jnp.dot(
                        rows[column, :, s * tile_side : (s + 1) * tile_side],
                        same_behind(block, column, s),
                        preferred_element_type=jnp.float32,
                    )
        weighted[block] = total

    def repeat(count, one):
        if count == 1:
            one(0)
        else:

            def step(place, carried):
                one(place)
                return carried

            lax.fori_loop(0, count, step, 0)

    def spread_at(ref, group, s):
        return ref[group * SUB : (group + 1) * SUB, s * tile_side : (s + 1) * tile_side]

    for copy in small:
        copy.wait()
    holds = [index_ref[0, slot] * row_count + index_ref[1, slot] for slot in range(slot_total)]

    def find_slot(position, carried):
        found = jnp.int32(-1)
        for slot in range(slot_total):
            found = jnp.where(holds[slot] == position, jnp.int32(slot), found)
        place_ref[position] = found
        return carried

    lax.fori_loop(0, positions, find_slot, 0)

    lane = lax.broadcasted_iota(jnp.int32, wide, 1)
    sub = lax.broadcasted_iota(jnp.int32, wide, 0)
    load.wait()

    band_base = my_row * col_count * tile_side

    part_row = lax.broadcasted_iota(jnp.int32, pick.shape, 0)
    part_source = lax.broadcasted_iota(jnp.int32, pick.shape, 1) // tile_side
    chosen = (part_row % source_rows == part_source) & (part_row < 3 * source_rows)
    pick[...] = jnp.where(chosen, 1.0 / scale_up, 0.0).astype(jnp.bfloat16)

    def first_level(column, carried):
        best = jnp.full(wide, far_value, jnp.float32)
        for row in range(source_rows):
            place = source_ref[row] - band_base
            inside = (place >= 0) & (place < col_count * tile_side)
            place = jnp.clip(place, 0, col_count * tile_side - 1)
            slot = place_ref[(place // tile_side) * row_count + column]
            line = raw[jnp.maximum(slot, 0), pl.ds(place % tile_side, 1), :]
            limit = jnp.where(inside & (slot >= 0), 0.0, far_value).astype(jnp.float32)
            best = jnp.where((sub == row) & (line > limit), line, best)
        dist_out[0, column] = best
        return carried

    lax.fori_loop(0, row_count, first_level, 0)
    dist_in[0, my_col, my_row] = dist_out[0, my_row]
    pl.semaphore_wait(barrier, row_count * col_count - 1)
    push_all(0, lambda other_row, other_col: dist_out.at[0, other_row], dist_in.at[0, my_col, my_row])

    def prepare(position, carried):
        slot = place_ref[position]
        tile = raw[jnp.maximum(slot, 0)]
        limit = jnp.where(slot >= 0, 0.0, far_value).astype(jnp.float32)
        weights[position] = jnp.where(tile > limit, tile, no_edge)
        return carried

    lax.fori_loop(0, positions, prepare, 0)

    def turn(position, carried):
        weights_back[position] = weights[position].T
        return carried

    lax.fori_loop(0, positions, turn, 0)

    def relax(block):
        near = lanes.at[block]

        def columns(chunk):
            first = chunk * row_chunk
            for s in range(source_rows):
                best = [gathered[first + t, s] for t in range(row_chunk)]
                for group in range(groups):
                    value = spread_at(near, group, s)
                    for t in range(row_chunk):
                        line = weights[
                            block * row_count + first + t, group * SUB : (group + 1) * SUB, :
                        ]
                        best[t] = jnp.minimum(best[t], value + line)
                for t in range(row_chunk):
                    gathered[first + t, s] = best[t]

        repeat(row_count // row_chunk, columns)

    def relax_column(level, block, column):
        near = lanes.at[block]
        best = [gathered[column, s] for s in range(source_rows)]
        for group in range(groups):
            line = weights[block * row_count + column, group * SUB : (group + 1) * SUB, :]
            for s in range(source_rows):
                best[s] = jnp.minimum(best[s], spread_at(near, group, s) + line)
        dist_out[level, column] = fold(best, jnp.minimum, sub)

    def tally(level, block, shares):
        def columns(chunk):
            for first in range(0, row_chunk, row_pair):
                tally_pair(level, block, shares, chunk * row_chunk + first)

        repeat(row_count // row_chunk, columns)

    def tally_pair(level, block, shares, first):
        total = [[gathered[first + t, s] for s in range(source_rows)] for t in range(row_pair)]
        best = [
            [
                jnp.broadcast_to(dist_out[level, first + t, s : s + 1, :], (SUB, tile_side))
                for s in range(source_rows)
            ]
            for t in range(row_pair)
        ]
        for group in range(groups):
            lines = [
                weights[block * row_count + first + t, group * SUB : (group + 1) * SUB, :]
                for t in range(row_pair)
            ]
            for s in range(source_rows):
                near = spread_at(lanes.at[block], group, s)
                paths = 1.0 if shares is None else spread_at(shares, group, s)
                for t in range(row_pair):
                    total[t][s] += jnp.where(near + lines[t] == best[t][s], paths, 0.0)
        for t in range(row_pair):
            for s in range(source_rows):
                gathered[first + t, s] = total[t][s]

    def same_behind(block, column, s):
        below = lanes[column, :, s * tile_side : (s + 1) * tile_side]
        upper = band[block, s : s + 1, :]
        same = upper + weights_back[block * row_count + column] == below
        return jnp.where(same, 1.0, 0.0).astype(jnp.bfloat16)

    def fill(count, value):
        def one(place, carried):
            for s in range(source_rows):
                gathered[place, s] = jnp.full((SUB, tile_side), value, jnp.float32)
            return carried

        lax.fori_loop(0, count, one, 0)

    def block_source(block):
        return source_mask((my_row * col_count + block) * tile_side)

    def spread_dist(level, block):
        best = nearest([dist_in[level - 1, block, g] for g in range(row_count)])
        spread(jnp.where(block_source(block), 0.0, best), lanes.at[block])

    def wait_count(block, own):
        block_arrived(LEVELS, count_in, block, own)

    def spread_count(level, block, target):
        found = combine(
            [dist_in[level - 1, block, g] for g in range(row_count)],
            [count_in[block, g] for g in range(row_count)],
        )
        spread(settle(*found, block_source(block))[1], target)

    def forward(level):
        fill(row_count, far_value)
        final = partner(my_col, col_count - 1, col_count)

        def relax_block(step, carried):
            block = partner(my_col, step, col_count)
            block_arrived(level - 1, dist_in.at[level - 1], block, step == 0)
            spread_dist(level, block)
            relax(block)
            return carried

        lax.fori_loop(0, col_count - 1, relax_block, 0)
        block_arrived(level - 1, dist_in.at[level - 1], final, None if col_count > 1 else True)
        if level > 1:
            wait_count(my_col, True)
        spread_dist(level, final)
        if level > 1:
            spread_count(level, my_col, lanes_even)
        for row_step in reversed(range(row_count)):
            column = partner(my_row, row_step, row_count)
            relax_column(level, final, column)
            for col_step in reversed(range(col_count)):
                if (row_step or col_step) and (col_step or level != last):
                    start(
                        dist_out.at[level, column],
                        dist_in.at[level, my_col, my_row],
                        all_send.at[level, row_step, col_step],
                        all_recv.at[level, my_row, my_col],
                        {"row": column, "col": partner(my_col, col_step, col_count)},
                    )
        if level == last:
            push_full(0, dist_out.at[level], full_dist)
        else:
            dist_in[level, my_col, my_row] = dist_out[level, my_row]

        fill(row_count, 0.0)
        if level > 1:

            def tally_next(step, shares, following_shares):
                following = partner(my_col, step + 1, col_count)
                wait_count(following, None)
                tally(level, partner(my_col, step, col_count), shares)
                spread_count(level, following, following_shares)

            def tally_two(pair):
                tally_next(2 * pair, lanes_even, lanes_odd)
                tally_next(2 * pair + 1, lanes_odd, lanes_even)

            if col_count > 2:
                repeat((col_count - 1) // 2, tally_two)
            if col_count % 2:
                tally(level, final, lanes_even)
            else:
                tally_next(col_count - 2, lanes_even, lanes_odd)
                tally(level, final, lanes_odd)
        else:

            def tally_block(block, carried):
                tally(level, block, None)
                return carried

            lax.fori_loop(0, col_count, tally_block, 0)

        def close_count(column, carried):
            total = fold([gathered[column, s] for s in range(source_rows)], jnp.add, sub)
            if level == 1:
                total = jnp.where(dist_out[level, column] < half_far, total, 0.0)
            count_out[level - 1, column] = total
            return carried

        lax.fori_loop(0, row_count, close_count, 0)
        if level == last:
            push_full(1, count_out.at[level - 1], full_count)
        else:
            count_in[my_col, my_row] = count_out[level - 1, my_row]
            push_all(
                LEVELS,
                lambda other_row, other_col: count_out.at[level - 1, other_row],
                count_in.at[my_col, my_row],
            )

    for level in range(1, LEVELS):
        forward(level)

    full_arrived(0, full_dist)

    own_best = nearest([full_dist[g, my_row] for g in range(row_count)])
    band[my_col] = jnp.where(block_source(my_col), 0.0, own_best)

    def lower_dist(chunk):
        for t in range(row_chunk):
            column = chunk * row_chunk + t
            best = nearest([full_dist[g, column] for g in range(row_count)])
            is_source = source_mask((column * col_count + my_col) * tile_side)
            settled = jnp.where(is_source, 0.0, best)
            lower[0, column] = settled
            spread(settled, lanes.at[column])
        for t in range(row_chunk if keep_masks else 0):
            column = chunk * row_chunk + t
            for s in range(source_rows):
                masks[my_col, column, s * tile_side : (s + 1) * tile_side, :] = same_behind(
                    my_col, column, s
                )

    repeat(row_count // row_chunk, lower_dist)

    def settle_upper(block):
        for row_step in range(row_count):
            giver = partner(my_row, row_step, row_count)
            arrived(
                dist_in.at[last, block, giver],
                all_recv.at[last, giver, block],
                {"row": giver, "col": block},
            )
        best = nearest([dist_in[last, block, g] for g in range(row_count)])
        is_source = source_mask((my_row * col_count + block) * tile_side)
        band[block] = jnp.where(is_source, 0.0, best)

    for col_step in range(1, col_count):
        block = partner(my_col, col_step, col_count)
        settle_upper(block)
        if keep_masks:

            def keep(column, carried, block=block):
                for s in range(source_rows):
                    masks[block, column, s * tile_side : (s + 1) * tile_side, :] = same_behind(
                        block, column, s
                    )
                return carried

            lax.fori_loop(0, row_count, keep, 0)

    def coefficient(column, dependency):
        paths = lower[1, column]
        deal(
            jnp.where(paths > 0.5, (1.0 + dependency) / jnp.maximum(paths, 1.0), 0.0),
            rows.at[column],
        )

    full_arrived(1, full_count)

    def lower_paths(chunk, carried):
        for t in range(row_chunk):
            column = chunk * row_chunk + t
            found = combine(
                [full_dist[g, column] for g in range(row_count)],
                [full_count[g, column] for g in range(row_count)],
            )
            is_source = source_mask((column * col_count + my_col) * tile_side)
            lower[1, column] = settle(*found, is_source)[1]
            coefficient(column, 0.0)
        return carried

    lax.fori_loop(0, row_count // row_chunk, lower_paths, 0)

    weighted[...] = jnp.zeros_like(weighted)
    for col_step in reversed(range(col_count)):
        block = partner(my_col, col_step, col_count)

        def first_sums(chunk, block=block):
            add_weighted([chunk * row_chunk + t for t in range(row_chunk)], block)

        repeat(row_count // row_chunk, first_sums)
        sums_out[0, block] = join(block)
        for row_step in reversed(range(row_count)):
            if row_step or col_step:
                other = partner(my_row, row_step, row_count)
                start(
                    sums_out.at[0, block],
                    sums_all.at[my_row, my_col],
                    all_send.at[LEVELS + 1, row_step, col_step],
                    all_recv.at[LEVELS + 1, my_row, my_col],
                    {"row": other, "col": block},
                )
            else:
                sums_all[my_row, my_col] = sums_out[0, block]

    packed[0] = jnp.where(lower[0, my_row] < half_far, lower[0, my_row], -1.0)
    packed[1] = lower[1, my_row]
    weighted[...] = jnp.zeros_like(weighted)

    def settle_columns(pair, own):
        columns = [partner(my_row, pair * row_pair + t, row_count) for t in range(row_pair)]
        for t, column in enumerate(columns):
            for col_step in range(col_count):
                giver = partner(my_col, col_step, col_count)

                def wait(column=column, giver=giver):
                    arrived(
                        sums_all.at[column, giver],
                        all_recv.at[LEVELS + 1, column, giver],
                        {"row": column, "col": giver},
                    )

                if col_step == 0 and t == 0 and own is not None:
                    pl.when(jnp.logical_not(own))(wait)
                else:
                    wait()
        for column in columns:
            summed = functools.reduce(jnp.add, [sums_all[column, g] for g in range(col_count)])
            coefficient(column, lower[1, column] * summed)
        return columns

    def from_columns(pair, carried):
        columns = settle_columns(pair, pair == 0)

        def some_blocks(chunk):
            for t in range(col_chunk):
                add_weighted(columns, chunk * col_chunk + t)

        repeat(col_count // col_chunk, some_blocks)
        return carried

    pairs = row_count // row_pair
    lax.fori_loop(0, pairs - 1, from_columns, 0)
    columns = settle_columns(pairs - 1, None if pairs > 1 else True)
    early = len(pending)
    for col_step in reversed(range(col_count)):
        block = partner(my_col, col_step, col_count)
        add_weighted(columns, block)
        sums_out[1, block] = join(block)
        if col_step:
            start(
                sums_out.at[1, block],
                sums_in.at[my_col],
                col_send.at[col_step],
                col_recv.at[my_col],
                {"row": my_row, "col": block},
            )
    for copy in pending[:early]:
        copy.wait_send()
    summed = sums_out[1, my_col]
    for col_step in range(1, col_count):
        other = partner(my_col, col_step, col_count)
        arrived(sums_in.at[other], col_recv.at[other], {"row": my_row, "col": other})
        summed += sums_in[other]
    own_source = source_mask((my_row * col_count + my_col) * tile_side)
    packed[2] = jnp.where(own_source, 0.0, lower[1, my_row] * summed)
    for copy in pending[early:]:
        copy.wait_send()


def unpack(packed, dist_out, path_out, cent_out):
    dist_out[...] = packed[0]
    path_out[...] = packed[1]
    cent_out[...] = jnp.sum(packed[2], axis=0, keepdims=True) / packed.shape[1]


def solution(mesh):
    row_count = mesh.shape["row"]
    col_count = mesh.shape["col"]

    def per_device(tiles, tile_index, tile_count, sources):
        del tile_count
        slot_total, tile_side = tiles.shape[0], tiles.shape[1]
        source_rows = sources.shape[0]
        wide = (source_rows, tile_side)
        positions = row_count * col_count
        longest = max(row_count, col_count)
        mask_shape = (col_count, row_count, source_rows * tile_side, tile_side)
        if positions > MASK_TILES:
            mask_shape = (1, 1, 2 * SUB, tile_side)
        vector = pl.BlockSpec(memory_space=pltpu.VMEM)
        packed = pl.pallas_call(
            functools.partial(body, row_count, col_count),
            out_shape=pltpu.VMEM((3,) + wide, jnp.float32),
            in_specs=[pl.BlockSpec(memory_space=pl.ANY)] * 3,
            out_specs=vector,
            scratch_shapes=[
                pltpu.SMEM((2, slot_total), jnp.int32),
                pltpu.SMEM((source_rows,), jnp.int32),
                pltpu.VMEM((slot_total, tile_side, tile_side), jnp.float32),
                pltpu.SMEM((positions,), jnp.int32),
                pltpu.VMEM((positions, tile_side, tile_side), jnp.float32),
                pltpu.VMEM((positions, tile_side, tile_side), jnp.float32),
                pltpu.VMEM((4 * source_rows, source_rows * tile_side), jnp.bfloat16),
                pltpu.VMEM((longest, tile_side, source_rows * tile_side), jnp.float32),
                pltpu.VMEM((tile_side, source_rows * tile_side), jnp.float32),
                pltpu.VMEM((tile_side, source_rows * tile_side), jnp.float32),
                pltpu.VMEM((longest, 4 * source_rows, source_rows * tile_side), jnp.bfloat16),
                pltpu.VMEM(mask_shape, jnp.bfloat16),
                pltpu.VMEM((col_count, 4 * source_rows, tile_side), jnp.float32),
                pltpu.VMEM((longest, source_rows, SUB, tile_side), jnp.float32),
                pltpu.VMEM((LEVELS, row_count) + wide, jnp.float32),
                pltpu.VMEM((LEVELS - 1, row_count) + wide, jnp.float32),
                pltpu.VMEM((LEVELS, col_count, row_count) + wide, jnp.float32),
                pltpu.VMEM((col_count, row_count) + wide, jnp.float32),
                pltpu.VMEM((row_count, row_count) + wide, jnp.float32),
                pltpu.VMEM((row_count, row_count) + wide, jnp.float32),
                pltpu.VMEM((col_count,) + wide, jnp.float32),
                pltpu.VMEM((2, row_count) + wide, jnp.float32),
                pltpu.VMEM((BACK, col_count) + wide, jnp.float32),
                pltpu.VMEM((row_count, col_count) + wide, jnp.float32),
                pltpu.VMEM((col_count,) + wide, jnp.float32),
                pltpu.SemaphoreType.DMA,
                pltpu.SemaphoreType.DMA((2,)),
                pltpu.SemaphoreType.DMA((LEVELS + 2, row_count, col_count)),
                pltpu.SemaphoreType.DMA((LEVELS + 2, row_count, col_count)),
                pltpu.SemaphoreType.DMA((2, row_count)),
                pltpu.SemaphoreType.DMA((2, row_count)),
                pltpu.SemaphoreType.DMA((col_count,)),
                pltpu.SemaphoreType.DMA((col_count,)),
            ],
            compiler_params=pltpu.CompilerParams(
                collective_id=0,
                has_side_effects=True,
            ),
        )(tile_index.T, sources, tiles)
        distance, paths, centrality = pl.pallas_call(
            unpack,
            out_shape=(
                jax.ShapeDtypeStruct(wide, jnp.float32),
                jax.ShapeDtypeStruct(wide, jnp.float32),
                jax.ShapeDtypeStruct((1, tile_side), jnp.float32),
            ),
            in_specs=[vector],
            out_specs=(vector, vector, vector),
            compiler_params=pltpu.CompilerParams(vmem_limit_bytes=2**20),
        )(packed)
        return distance, paths, centrality.reshape(tile_side)

    in_specs = (
        P(("groups", "row", "col"), None, None),
        P(("groups", "row", "col"), None),
        P(("groups", "row", "col")),
        P("groups"),
    )
    out_specs = (
        P("groups", ("row", "col")),
        P("groups", ("row", "col")),
        P(("groups", "row", "col")),
    )
    return jax.shard_map(
        per_device, mesh=mesh, in_specs=in_specs, out_specs=out_specs, check_vma=False
    )
```
